128 devices in a mesh: row: 16 (over x, z), col: 8 (over y, core).
Axes of the slice: x: 4, y: 4, z: 4, core: 2. Of those that a mesh axis runs over, the one named last changes fastest.
Arguments:
- tiles: bfloat16 [768, 1024, 1024], P(('row', 'col')), may hold values from -0.1875 to 0.1875
- tile_list: int32 [768, 2], P(('row', 'col')), may hold values from 0 to 63, as said below
- tile_count: int32 [128], P(('row', 'col')), may hold values from 1 to 6, as said below
- scale_index: int32 [768], P(('row', 'col')), may hold values from 0 to 63
- scales: float32 [64], replicated, may hold values from 0.25 to 4
- panel_start: bfloat16 [65536, 128], P(('row', 'col')), may hold values from -6 to 6
- centroids: bfloat16 [4096, 128], replicated, may hold values from -2 to 2
Outputs:
- panel: bfloat16 [65536, 128], P(('row', 'col'))
- centers: float32 [4096, 128], replicated
The draws below stay inside these ranges and needn't reach their ends.
Inputs may be any that keep to these rules, and one draw needn't show every extreme that they name: `tile_list`: device d holds slots d * 6 to (d + 1) * 6 - 1. With d = i * 8 + j, its tiles lie in row blocks i * 4 to (i + 1) * 4 - 1 and column blocks j * 8 to (j + 1) * 8 - 1, and no two slots of a device name the same block. `tile_count`: live slots of each device; some device fills all its slots.
All inputs are finite; a program needn't handle non-finite values.
Results may differ from the reference program's by a relative error of at most 0.008.
Values may be sent and summed in bfloat16 or wider, within the bound.
No kernel may reach another device: no remote copies, remote signals or barrier semaphores. Data moves between devices by JAX's collectives and lax.ppermute only.
A program may use at most 128 MiB of HBM per device.

```python
import math
import jax
import jax.numpy as jnp
from jax import lax

BLOCK = 1024
RANK = 128
CENTROIDS = 4096
ROWS_DEV = 512
SLOT_DEV = 6
ROUNDS = 2
SCALES = 64
ROWS = 65536
SLOTS = 768
BROWS = 4
BCOLS = 8
N_COL = 8
DEVICES = 128


def draw_tile_list(key, part):
    cells = BROWS * BCOLS
    noise = jax.random.randint(jax.random.fold_in(key, 11), (DEVICES, cells), 0, 65536)
    keyed = noise * cells + jnp.arange(cells, dtype=jnp.int32)[None, :]
    chosen = jnp.argsort(keyed, axis=1)[:, :SLOT_DEV].astype(jnp.int32)
    device = jnp.arange(DEVICES, dtype=jnp.int32)[:, None]
    row_block = device // N_COL * BROWS + chosen // BCOLS
    col_block = device % N_COL * BCOLS + chosen % BCOLS
    return jnp.stack([row_block, col_block], axis=-1).reshape(SLOTS, 2).astype(jnp.int32)


def draw_tile_count(key, part):
    first = jax.random.randint(jax.random.fold_in(key, 21), (DEVICES,), 1, SLOT_DEV + 1)
    second = jax.random.randint(jax.random.fold_in(key, 22), (DEVICES,), 1, SLOT_DEV + 1)
    busiest = jax.random.randint(jax.random.fold_in(key, 23), (), 0, DEVICES)
    counts = jnp.minimum(first, second)
    return jnp.where(jnp.arange(DEVICES, dtype=jnp.int32) == busiest, SLOT_DEV, counts).astype(jnp.int32)


def draw_centroids(key, part):
    unit = RANK ** (-0.5)
    values = jnp.clip(jax.random.normal(jax.random.fold_in(key, 33), (CENTROIDS, RANK), jnp.float32), -4.0, 4.0) * unit
    return values.astype(jnp.bfloat16)


def touch_ends(array, key, least, largest):
    shape = array.shape
    place = [jax.random.randint(jax.random.fold_in(key, axis), (), 0, shape[axis]) for axis in range(len(shape))]
    array = array.at[tuple(place)].set(least)
    longest = shape.index(max(shape))
    place[longest] = (place[longest] + 1) % shape[longest]
    return array.at[tuple(place)].set(largest)


def shard_levels(stream_key, dims, split, smallest, high):
    def one(axis_at, blocks):
        steps = jax.random.uniform(jax.random.fold_in(jax.random.fold_in(stream_key, 6), axis_at), (blocks,), jnp.float32, smallest / len(split), high / len(split))
        return jnp.repeat(jnp.exp(steps), dims[axis_at] // blocks).reshape((-1,) + (1,) * (len(dims) - axis_at - 1))

    loudness = one(*split[0])
    for cut in split[1:]:
        loudness = loudness * one(*cut)
    return loudness


def scatter_about(own_key, shape, deviation, reach, shards=(), kind=jnp.bfloat16):
    values = jax.random.normal(own_key, shape, jnp.float32) * deviation
    if len(shards) > 0:
        values = shard_levels(own_key, shape, shards, -0.22, 0.18) * values
    return jnp.clip(values, min=-reach, max=reach).astype(kind)


def setup_inputs(seed: int = 0) -> dict:
    key_list = jax.random.split(jax.random.key(seed), 8)
    return {
        "tiles": scatter_about(key_list[0], (SLOTS, BLOCK, BLOCK), BLOCK ** -0.5, 0.1875, ((0, 128),)),
        "tile_list": draw_tile_list(jax.random.fold_in(key_list[7], 71), 0),
        "tile_count": draw_tile_count(jax.random.fold_in(key_list[7], 71), 0),
        "scale_index": touch_ends(jax.random.randint(key_list[3], (SLOTS,), 0, SCALES), jax.random.fold_in(key_list[3], 1), 0, SCALES - 1).astype(jnp.int32),
        "scales": jnp.clip(jnp.exp(jax.random.uniform(key_list[4], (SCALES,), jnp.float32, math.log(0.25), math.log(4.0))), 0.25, 4.0),
        "panel_start": scatter_about(key_list[5], (ROWS, RANK), 1.0, 6.0, ((0, 128),)),
        "centroids": draw_centroids(jax.random.fold_in(key_list[7], 71), 0),
    }


SHARPNESS = 48.0
EPS = 1e-06

def multiply(tiles, source_blocks, target_blocks, live, weights, panel_in, transposed):
    block_size = tiles.shape[1]

    def step(running, item):
        tile_data, source, target, alive, weight = item

        def add_tile(current_sum):
            source_rows = lax.dynamic_slice_in_dim(panel_in, source * block_size, block_size, 0)
            if transposed:
                product_block = lax.dot_general(tile_data.astype(jnp.float32), source_rows.astype(jnp.float32), (((0,), (0,)), ((), ())), preferred_element_type=jnp.float32)
            else:
                product_block = jnp.dot(tile_data.astype(jnp.float32), source_rows.astype(jnp.float32), preferred_element_type=jnp.float32)
            offset = target * block_size
            current = lax.dynamic_slice_in_dim(current_sum, offset, block_size, 0)
            return lax.dynamic_update_slice_in_dim(current_sum, current + weight * product_block, offset, 0)
        return (lax.cond(alive, add_tile, lambda current_sum: current_sum, running), None)
    start_sum = jnp.zeros((ROWS, RANK), jnp.float32)
    running, _ = lax.scan(step, start_sum, (tiles, source_blocks, target_blocks, live, weights))
    return running

def orthonormal(product):
    gram_matrix = lax.dot_general(product.astype(jnp.float32), product.astype(jnp.float32), (((0,), (0,)), ((), ())), precision=lax.Precision.HIGHEST, preferred_element_type=jnp.float32) / ROWS
    lower_factor = jnp.linalg.cholesky(gram_matrix)
    identity = jnp.eye(RANK, dtype=jnp.float32)
    inverse = lax.linalg.triangular_solve(lower_factor, identity, left_side=True, lower=True)
    return jnp.dot(product.astype(jnp.float32), inverse.T.astype(jnp.float32), precision=lax.Precision.HIGHEST, preferred_element_type=jnp.float32).astype(jnp.bfloat16)

def reference(tiles, tile_list, tile_count, scale_index, scales, panel_start, centroids):
    slot_ids = jnp.arange(SLOTS, dtype=jnp.int32)
    live = slot_ids % SLOT_DEV < tile_count[slot_ids // SLOT_DEV]
    weights = scales[scale_index]
    row_blocks = tile_list[:, 0]
    col_blocks = tile_list[:, 1]
    panel = panel_start
    for round_index in range(ROUNDS):
        product = multiply(tiles, row_blocks, col_blocks, live, weights, panel, True)
        factor = orthonormal(product)
        product = multiply(tiles, col_blocks, row_blocks, live, weights, factor, False)
        panel = orthonormal(product)
    center_values = centroids.astype(jnp.float32)
    center_sq = lax.optimization_barrier(jnp.sum(center_values * center_values, axis=1))

    def cluster(carry, rows_block):
        sums, totals = carry
        values = rows_block.astype(jnp.float32)
        row_norm = jnp.sqrt(lax.optimization_barrier(jnp.sum(values * values, axis=1, keepdims=True)) + EPS)
        points = (values / row_norm).astype(jnp.bfloat16)
        affinity = lax.dot_general(points.astype(jnp.float32), centroids.astype(jnp.float32), (((1,), (1,)), ((), ())), preferred_element_type=jnp.float32)
        scores = SHARPNESS * (2.0 * affinity - center_sq[None, :])
        shifted = jnp.exp(scores - lax.optimization_barrier(jnp.max(scores, axis=1, keepdims=True)))
        resp = (shifted / lax.optimization_barrier(jnp.sum(shifted, axis=1, keepdims=True))).astype(jnp.bfloat16)
        sums = sums + lax.dot_general(resp.astype(jnp.float32), points.astype(jnp.float32), (((0,), (0,)), ((), ())), preferred_element_type=jnp.float32)
        totals = totals + lax.optimization_barrier(jnp.sum(resp.astype(jnp.float32), axis=0))
        return ((sums, totals), None)
    blocks = panel.reshape(ROWS // ROWS_DEV, ROWS_DEV, RANK)
    start_carry = (jnp.zeros((CENTROIDS, RANK), jnp.float32), jnp.zeros((CENTROIDS,), jnp.float32))
    (sums, totals), _ = lax.scan(cluster, start_carry, blocks)
    centers = (sums + center_values) / (totals[:, None] + 1.0)
    return (panel, centers)
```

```python
import jax
import jax.numpy as jnp
from jax import lax
from jax.experimental import pallas as pl
from jax.experimental.pallas import tpu as pltpu
from jax.sharding import PartitionSpec as P

ROUNDS = 2
SHARPNESS = 48.0
EPS = 1e-06

SIDE = 4
BF = jnp.bfloat16
F32 = jnp.float32
HIGHEST = lax.Precision.HIGHEST


def dot(a, b, contract, precision=None):
    return lax.dot_general(
        a, b, ((contract[:1], contract[1:]), ((), ())), precision=precision,
        preferred_element_type=F32,
    )


def shift_row(value, dx, dz):
    pairs = [
        (x * SIDE + z, (x + dx) % SIDE * SIDE + (z + dz) % SIDE)
        for x in range(SIDE)
        for z in range(SIDE)
    ]
    return lax.ppermute(value, "row", pairs)


def shift_col(value, dy, dc):
    pairs = [
        (y * 2 + c, (y + dy) % SIDE * 2 + (c + dc) % 2) for y in range(SIDE) for c in range(2)
    ]
    return lax.ppermute(value, "col", pairs)


def sum_row(value):
    value = value + shift_row(value, 1, 0) + shift_row(value, 2, 0) + shift_row(value, 3, 0)
    return value + shift_row(value, 0, 1) + shift_row(value, 0, 2) + shift_row(value, 0, 3)


def sum_col(value):
    value = value + shift_col(value, 1, 0) + shift_col(value, 2, 0) + shift_col(value, 3, 0)
    return value + shift_col(value, 0, 1)


def whole(shape):
    return pl.BlockSpec(shape, lambda *_: (0,) * len(shape))


def small_call(body, name, out_shapes, *args):
    return pl.pallas_call(body, out_shape=out_shapes, name=name)(*args)


def down_body(meta, weights, mine, theirs, tile, out, acc, rows):
    step = pl.program_id(0)
    half = mine.shape[1]

    @pl.when(step == 0)
    def _():
        acc[...] = jnp.zeros_like(acc)

    @pl.when(step < meta[12])
    def _():
        place = (meta[13] + SIDE - meta[step]) % SIDE
        core = meta[14]
        rows[pl.ds(pl.multiple_of(core * half, half), half), :] = mine[place]
        rows[pl.ds(pl.multiple_of((1 - core) * half, half), half), :] = theirs[place]
        product = dot(rows[...], tile[0], (0, 0))
        target = meta[6 + step]
        acc[target] = acc[target] + weights[step] * product

    @pl.when(step == pl.num_programs(0) - 1)
    def _():
        for block in range(acc.shape[0]):
            out[2 * block] = acc[block, :, :half].astype(BF)
            out[2 * block + 1] = acc[block, :, half:].astype(BF)


def up_body(meta, weights, gathered, tile, keep, send, acc):
    step = pl.program_id(0)
    half = gathered.shape[2]

    @pl.when(step == 0)
    def _():
        acc[...] = jnp.zeros_like(acc)

    @pl.when(step < meta[12])
    def _():
        source = meta[6 + step]
        product = dot(tile[0, :, :half], gathered[2 * source], (1, 1))
        product += dot(tile[0, :, half:], gathered[2 * source + 1], (1, 1))
        target = meta[step]
        acc[target] = acc[target] + weights[step] * product

    @pl.when(step == pl.num_programs(0) - 1)
    def _():
        core = meta[14]
        for block in range(acc.shape[0]):
            keep[block] = acc[block, pl.ds(pl.multiple_of(core * half, half), half), :]
            send[block] = acc[block, pl.ds(pl.multiple_of((1 - core) * half, half), half), :]


def tile_call(body, name, meta, weights, panels, tiles, outs, scratch):
    slots, block, _ = tiles.shape
    rank = 128
    grid_spec = pltpu.PrefetchScalarGridSpec(
        num_scalar_prefetch=1,
        grid=(slots,),
        in_specs=[pl.BlockSpec(memory_space=pltpu.SMEM)]
        + [pl.BlockSpec(p.shape, lambda i, meta, n=p.ndim: (0,) * n) for p in panels]
        + [pl.BlockSpec((1, block, block), lambda i, meta: (jnp.minimum(i, meta[12] - 1), 0, 0))],
        out_specs=[pl.BlockSpec(o.shape, lambda i, meta, n=len(o.shape): (0,) * n) for o in outs],
        scratch_shapes=scratch,
    )
    return pl.pallas_call(
        body,
        grid_spec=grid_spec,
        out_shape=outs,
        name=name,
        cost_estimate=pl.CostEstimate(
            flops=2 * slots * block * block * rank,
            transcendentals=0,
            bytes_accessed=slots * block * block * 2 + 4 * 1024 * 1024,
        ),
    )(meta, weights, *panels, tiles)


def reduce_first_body(parts, out):
    out[...] = jnp.sum(parts[...].astype(F32), axis=0).astype(BF)


def reduce_down_body(parts, inverse, out):
    total = jnp.sum(parts[...].astype(F32), axis=0)
    out[...] = dot(inverse[...], total, (1, 0), HIGHEST).astype(BF)


def fold_body(where, keep, got, own, one, two, three):
    at = where[0]
    own[...] = keep[at] + got[at]
    for distance, out in ((1, one), (2, two), (3, three)):
        to = (at + distance) % SIDE
        out[...] = (keep[to] + got[to]).astype(BF)


def reduce_up_body(own, one, two, three, inverse, out):
    total = own[...] + one[...].astype(F32) + two[...].astype(F32) + three[...].astype(F32)
    out[...] = dot(total, inverse[...], (1, 1), HIGHEST).astype(BF)


def reduce_last_body(own, one, two, three, inverse, out, gram):
    total = own[...] + one[...].astype(F32) + two[...].astype(F32) + three[...].astype(F32)
    total = dot(total, inverse[...], (1, 1), HIGHEST)
    out[...] = total
    gram[...] = dot(total, total, (0, 0), HIGHEST)


def gram_wide_body(parts, out):
    total = jnp.zeros(out.shape, F32)
    for part in range(parts.shape[0]):
        total += dot(parts[part], parts[part], (1, 1))
    out[...] = total


def gram_tall_body(mine, theirs, out):
    total = jnp.zeros(out.shape, F32)
    for part in range(mine.shape[0]):
        total += dot(mine[part], mine[part], (0, 0))
        total += dot(theirs[part], theirs[part], (0, 0))
    out[...] = total


def inverse_factor(gram, total_rows):
    lower = jnp.linalg.cholesky(gram / total_rows)
    identity = jnp.eye(gram.shape[0], dtype=F32)
    return lax.linalg.triangular_solve(lower, identity, left_side=True, lower=True)


def cluster_body(product, inverse, centroids, panel, sums, totals, norms):
    step = pl.program_id(0)

    @pl.when(step == 0)
    def _():
        values = centroids[...].astype(F32)
        norms[...] = jnp.sum(values * values, axis=1, keepdims=True)
        sums[...] = jnp.zeros_like(sums)
        totals[...] = jnp.zeros_like(totals)

    rows = dot(product[...], inverse[...], (1, 1), HIGHEST).astype(BF)
    panel[...] = rows
    values = rows.astype(F32)
    length = jnp.sqrt(jnp.sum(values * values, axis=1, keepdims=True) + EPS)
    points = (values / length).astype(BF)
    affinity = dot(centroids[...], points, (1, 1))
    scores = SHARPNESS * (2.0 * affinity - norms[...])
    shifted = jnp.exp(scores - jnp.max(scores, axis=0, keepdims=True))
    resp = (shifted / jnp.sum(shifted, axis=0, keepdims=True)).astype(BF)
    sums[...] += dot(resp, points, (1, 0))
    totals[...] += dot(jnp.ones((8, resp.shape[1]), BF), resp, (1, 1))


def cluster(product, inverse, centroids, chunk):
    rows, rank = product.shape
    count = centroids.shape[0]
    return pl.pallas_call(
        cluster_body,
        grid=(rows // chunk,),
        in_specs=[
            pl.BlockSpec((chunk, rank), lambda i: (i, 0)),
            whole(inverse.shape),
            whole(centroids.shape),
        ],
        out_specs=[
            pl.BlockSpec((chunk, rank), lambda i: (i, 0)),
            whole((count, rank)),
            whole((8, count)),
        ],
        out_shape=[
            jax.ShapeDtypeStruct((rows, rank), BF),
            jax.ShapeDtypeStruct((count, rank), F32),
            jax.ShapeDtypeStruct((8, count), F32),
        ],
        scratch_shapes=[pltpu.VMEM((count, 1), F32)],
        name="cluster",
    )(product, inverse, centroids)


def pack_body(sums, totals, out):
    share = sums.shape[0] // out.shape[0]
    lanes = sums.shape[1]
    for piece in range(out.shape[0]):
        out[piece, :share, :] = sums[piece * share : (piece + 1) * share, :].astype(BF)
        ends = [
            totals[0:1, piece * share + k * lanes : piece * share + (k + 1) * lanes]
            for k in range(share // lanes)
        ]
        value = jnp.concatenate(ends, axis=0)
        high = value.astype(BF).astype(F32)
        tail = jnp.concatenate(
            [high, value - high, jnp.zeros((16 - 2 * len(ends), lanes), F32)], axis=0
        )
        out[piece, share:, :] = tail.astype(BF)


def gathered_sum_body(parts, out):
    out[...] = jnp.sum(parts[...].astype(F32), axis=0)


def centers_body(where, first, second, third, fourth, centroids, out):
    at = where[0]
    parts = (first, second, third, fourth)
    stack = [part[...] for part in parts]
    total = jnp.zeros_like(stack[0])
    for y in range(SIDE):
        place = (at + SIDE - y) % SIDE
        pick = stack[0]
        for k in range(1, SIDE):
            pick = jnp.where(place == k, stack[k], pick)
        total = total + pick
    share = out.shape[0]
    lanes = out.shape[1]
    mass = total[share : share + share // lanes] + total[share + share // lanes : share + 2 * (share // lanes)]
    for k in range(share // lanes):
        column = jnp.transpose(jnp.broadcast_to(mass[k : k + 1], (lanes, lanes)))
        block = slice(k * lanes, (k + 1) * lanes)
        out[block, :] = (
            (total[block] + centroids[block].astype(F32)) / (column + 1.0)
        ).astype(BF)


def shards(tiles, tile_list, tile_count, scale_index, scales, panel_start, centroids):
    block_size = tiles.shape[1]
    piece, rank = panel_start.shape
    rows_axis = lax.axis_size("row")
    cols_axis = lax.axis_size("col")
    total_rows = piece * rows_axis * cols_axis
    row_at = lax.axis_index("row")
    col_at = lax.axis_index("col")
    row_blocks = piece * cols_axis // block_size
    col_blocks = piece * rows_axis // block_size
    meta = jnp.concatenate(
        [
            tile_list[:, 0] - row_at * row_blocks,
            tile_list[:, 1] - col_at * col_blocks,
            tile_count,
            jnp.stack([col_at // 2, col_at % 2]).astype(jnp.int32),
        ]
    )
    where = (col_at // 2).astype(jnp.int32)[None]
    table_ids = jnp.arange(scales.shape[0], dtype=jnp.int32)
    weights = jnp.sum(
        jnp.where(scale_index[:, None] == table_ids[None, :], scales[None, :], 0.0), axis=1
    )
    square = jax.ShapeDtypeStruct((rank, rank), F32)
    tall = jax.ShapeDtypeStruct((piece, rank), BF)
    tall_f32 = jax.ShapeDtypeStruct((piece, rank), F32)
    wide = jax.ShapeDtypeStruct((rank, piece), BF)
    smem = pl.BlockSpec(memory_space=pltpu.SMEM)
    vmem = pl.BlockSpec(memory_space=pltpu.VMEM)

    panel = panel_start
    inverse = None
    for round_index in range(ROUNDS):
        mine = jnp.stack([panel] + [shift_col(panel, d, 0) for d in (1, 2, 3)])
        theirs = shift_col(mine, 0, 1)
        if round_index > 0:
            gram = sum_row(small_call(gram_tall_body, "gram_tall", square, mine, theirs))
            inverse = inverse_factor(gram, total_rows)
        (partial,) = tile_call(
            down_body, "down", meta, weights, [mine, theirs], tiles,
            [jax.ShapeDtypeStruct((rows_axis, rank, piece), BF)],
            [pltpu.VMEM((col_blocks, rank, block_size), F32), pltpu.VMEM((block_size, rank), BF)],
        )
        parts = lax.all_to_all(partial, "row", 0, 0, tiled=True)
        if inverse is None:
            factor = small_call(reduce_first_body, "reduce_first", wide, parts)
        else:
            factor = small_call(reduce_down_body, "reduce_down", wide, parts, inverse)
        copies = jnp.broadcast_to(factor[None], (rows_axis,) + factor.shape)
        gathered = lax.all_to_all(copies, "row", 0, 0, tiled=True)
        gram = sum_col(small_call(gram_wide_body, "gram_wide", square, gathered))
        inverse = inverse_factor(gram, total_rows)
        keep, send = tile_call(
            up_body, "up", meta, weights, [gathered], tiles,
            [jax.ShapeDtypeStruct((SIDE, piece, rank), F32)] * 2,
            [pltpu.VMEM((row_blocks, block_size, rank), F32)],
        )
        got = shift_col(send, 0, 1)
        own, one, two, three = pl.pallas_call(
            fold_body,
            in_specs=[smem, vmem, vmem],
            out_shape=[tall_f32, tall, tall, tall],
            name="fold",
        )(where, keep, got)
        one, two, three = shift_col(one, 1, 0), shift_col(two, 2, 0), shift_col(three, 3, 0)
        if round_index + 1 < ROUNDS:
            panel = small_call(reduce_up_body, "reduce_up", tall, own, one, two, three, inverse)
        else:
            product, gram = small_call(
                reduce_last_body, "reduce_last", [tall_f32, square], own, one, two, three, inverse
            )
    inverse = inverse_factor(sum_col(sum_row(gram)), total_rows)

    panel, sums, totals = cluster(product, inverse, centroids, 256)
    count = centroids.shape[0]
    share = count // rows_axis
    packed = small_call(
        pack_body, "pack", jax.ShapeDtypeStruct((rows_axis, share + 16, rank), BF), sums, totals
    )
    parts = lax.all_to_all(packed, "row", 0, 0, tiled=True)
    mass = small_call(
        gathered_sum_body, "mass", jax.ShapeDtypeStruct((share + 16, rank), F32), parts
    )
    mass = mass + shift_col(mass, 0, 1)
    owned = lax.dynamic_slice_in_dim(centroids, row_at * share, share, 0)
    centers = pl.pallas_call(
        centers_body,
        in_specs=[smem] + [vmem] * 5,
        out_shape=jax.ShapeDtypeStruct((share, rank), BF),
        name="centers",
    )(where, mass, shift_col(mass, 1, 0), shift_col(mass, 2, 0), shift_col(mass, 3, 0), owned)
    copies = jnp.broadcast_to(centers[None], (rows_axis,) + centers.shape)
    centers = lax.all_to_all(copies, "row", 0, 0, tiled=True)
    return (panel, centers.reshape(count, rank).astype(F32))


def solution(mesh):
    return jax.shard_map(
        shards,
        mesh=mesh,
        in_specs=(
            P(("row", "col"), None, None),
            P(("row", "col"), None),
            P(("row", "col")),
            P(("row", "col")),
            P(),
            P(("row", "col"), None),
            P(),
        ),
        out_specs=(P(("row", "col"), None), P()),
        check_vma=False,
    )
```

```python
import functools
import math

import jax
import jax.numpy as jnp
from jax import lax
from jax.experimental import pallas as pl
from jax.experimental.pallas import tpu as pltpu
from jax.sharding import PartitionSpec as P

ROUNDS = 2
SHARPNESS = 48.0
EPS = 1e-06
CLOSE = 1e-05

SIDE = 4
BF = jnp.bfloat16
F32 = jnp.float32
HIGHEST = lax.Precision.HIGHEST


def dot(a, b, contract, precision=None):
    return lax.dot_general(
        a, b, ((contract[:1], contract[1:]), ((), ())), precision=precision,
        preferred_element_type=F32,
    )


def shift_row(value, dx, dz):
    pairs = [
        (x * SIDE + z, (x + dx) % SIDE * SIDE + (z + dz) % SIDE)
        for x in range(SIDE)
        for z in range(SIDE)
    ]
    return lax.ppermute(value, "row", pairs)


def shift_col(value, dy, dc):
    pairs = [
        (y * 2 + c, (y + dy) % SIDE * 2 + (c + dc) % 2) for y in range(SIDE) for c in range(2)
    ]
    return lax.ppermute(value, "col", pairs)


def whole(shape):
    return pl.BlockSpec(shape, lambda *_: (0,) * len(shape))


def small_call(body, name, out_shapes, *args):
    return pl.pallas_call(body, out_shape=out_shapes, name=name)(*args)


def down_body(meta, weights, mine, theirs, tile, out, acc, rows):
    step = pl.program_id(0)
    half = mine.shape[1]

    @pl.when(step == 0)
    def _():
        acc[...] = jnp.zeros_like(acc)

    @pl.when(step < meta[12])
    def _():
        place = (meta[13] + SIDE - meta[step]) % SIDE
        core = meta[14]
        rows[pl.ds(pl.multiple_of(core * half, half), half), :] = mine[place]
        rows[pl.ds(pl.multiple_of((1 - core) * half, half), half), :] = theirs[place]
        product = dot(rows[...], tile[0], (0, 0))
        target = meta[6 + step]
        acc[target] = acc[target] + weights[step] * product

    @pl.when(step == pl.num_programs(0) - 1)
    def _():
        for block in range(acc.shape[0]):
            out[2 * block] = acc[block, :, :half].astype(BF)
            out[2 * block + 1] = acc[block, :, half:].astype(BF)


def up_body(meta, weights, gathered, tile, keep, send, acc):
    step = pl.program_id(0)
    half = gathered.shape[2]

    @pl.when(step == 0)
    def _():
        acc[...] = jnp.zeros_like(acc)

    @pl.when(step < meta[12])
    def _():
        source = meta[6 + step]
        product = dot(tile[0, :, :half], gathered[2 * source], (1, 1))
        product += dot(tile[0, :, half:], gathered[2 * source + 1], (1, 1))
        target = meta[step]
        acc[target] = acc[target] + weights[step] * product

    @pl.when(step == pl.num_programs(0) - 1)
    def _():
        core = meta[14]
        for block in range(acc.shape[0]):
            keep[block] = acc[block, pl.ds(pl.multiple_of(core * half, half), half), :]
            send[block] = acc[block, pl.ds(pl.multiple_of((1 - core) * half, half), half), :]


def tile_call(body, name, meta, weights, panels, tiles, outs, scratch):
    slots, block, _ = tiles.shape
    rank = 128
    grid_spec = pltpu.PrefetchScalarGridSpec(
        num_scalar_prefetch=1,
        grid=(slots,),
        in_specs=[pl.BlockSpec(memory_space=pltpu.SMEM)]
        + [pl.BlockSpec(p.shape, lambda i, meta, n=p.ndim: (0,) * n) for p in panels]
        + [pl.BlockSpec((1, block, block), lambda i, meta: (jnp.minimum(i, meta[12] - 1), 0, 0))],
        out_specs=[pl.BlockSpec(o.shape, lambda i, meta, n=len(o.shape): (0,) * n) for o in outs],
        scratch_shapes=scratch,
    )
    return pl.pallas_call(
        body,
        grid_spec=grid_spec,
        out_shape=outs,
        name=name,
        cost_estimate=pl.CostEstimate(
            flops=2 * slots * block * block * rank,
            transcendentals=0,
            bytes_accessed=slots * block * block * 2 + 4 * 1024 * 1024,
        ),
    )(meta, weights, *panels, tiles)


def share_wide(total, out, gram):
    factor = total.astype(BF)
    for copy in range(out.shape[0]):
        out[copy] = factor
    gram[...] = dot(factor, factor, (1, 1))


def reduce_first_body(parts, out, gram):
    share_wide(jnp.sum(parts[...].astype(F32), axis=0), out, gram)


def reduce_down_body(parts, upper, out, gram):
    total = jnp.sum(parts[...].astype(F32), axis=0)
    share_wide(dot(upper[...], total, (0, 0), HIGHEST), out, gram)


def fold_body(where, keep, got, own, one, two, three):
    at = where[0]
    own[...] = keep[at] + got[at]
    for distance, out in ((1, one), (2, two), (3, three)):
        to = (at + distance) % SIDE
        out[...] = (keep[to] + got[to]).astype(BF)


def reduce_up_body(own, one, two, three, upper, out, gram):
    total = own[...] + one[...].astype(F32) + two[...].astype(F32) + three[...].astype(F32)
    panel = dot(total, upper[...], (1, 0), HIGHEST).astype(BF)
    out[...] = panel
    gram[...] = dot(panel, panel, (0, 0))


def reduce_last_body(own, one, two, three, upper, out, gram):
    total = own[...] + one[...].astype(F32) + two[...].astype(F32) + three[...].astype(F32)
    total = dot(total, upper[...], (1, 0), HIGHEST)
    out[...] = total
    gram[...] = dot(total, total, (0, 0), HIGHEST)


def factor_body(total_rows, *refs):
    *grams, out, work, build = refs
    gram = sum(part[...] for part in grams) / total_rows
    size = gram.shape[0]
    down = lax.broadcasted_iota(jnp.int32, (size, size), 0)
    across = lax.broadcasted_iota(jnp.int32, (size, size), 1)
    eye = jnp.where(down == across, 1.0, 0.0).astype(F32)
    keep = jnp.where(down < across, 1.0, 0.5 * eye)
    diagonal = gram * eye
    tall = lax.rsqrt(jnp.sum(diagonal, axis=1, keepdims=True))
    scaled = gram * tall * lax.rsqrt(jnp.sum(diagonal, axis=0, keepdims=True))
    build[...] = eye - keep * (scaled - eye)

    def refine(state):
        at, _ = state
        guess = build[...]
        excess = dot(guess, dot(scaled, guess, (1, 0), HIGHEST), (0, 0), HIGHEST) - eye
        build[...] = guess - dot(guess, keep * excess, (1, 0), HIGHEST)
        return at + 1, jnp.max(jnp.abs(excess))

    def unfinished(state):
        at, error = state
        return (at < 10) & jnp.logical_not(error < CLOSE)

    _, error = lax.while_loop(unfinished, refine, (jnp.int32(0), jnp.float32(1.0)))
    out[...] = build[...] * tall

    @pl.when(jnp.logical_not(error < CLOSE))
    def _():
        work[...] = gram
        build[...] = eye

        def eliminate(k, carry):
            row = work[pl.ds(k, 1), :]
            pivot = jnp.sum(jnp.where(across[:1] == k, row, 0.0), axis=1, keepdims=True)
            column = jnp.sum(jnp.where(across == k, work[...], 0.0), axis=1, keepdims=True)
            ratio = jnp.where(down[:, :1] > k, column / pivot, 0.0)
            unit = build[pl.ds(k, 1), :]
            work[...] = work[...] - ratio * row
            build[...] = build[...] - ratio * unit
            return carry

        lax.fori_loop(0, size, eliminate, 0)
        pivots = jnp.sum(work[...] * eye, axis=1, keepdims=True)
        out[...] = jnp.transpose(build[...] * lax.rsqrt(pivots))


def ring_sum(value, shift):
    return value + shift(value, 1) + shift(value, 2) + shift(value, 3)


def sum_x(value):
    return ring_sum(value, lambda v, d: shift_row(v, d, 0))


def sum_z(value):
    return ring_sum(value, lambda v, d: shift_row(v, 0, d))


def sum_y(value):
    return ring_sum(value, lambda v, d: shift_col(v, d, 0))


def factor_of(total_rows, *grams):
    gram = grams[0]
    return pl.pallas_call(
        functools.partial(factor_body, total_rows),
        out_shape=jax.ShapeDtypeStruct(gram.shape, F32),
        scratch_shapes=[pltpu.VMEM(gram.shape, F32)] * 2,
        name="factor",
    )(*grams)


def cluster_body(product, upper, centroids, panel, packed, sums, totals, norms):
    step = pl.program_id(0)
    unit = SHARPNESS * math.log2(math.e)

    @pl.when(step == 0)
    def _():
        values = centroids[...].astype(F32)
        norms[...] = unit * jnp.sum(values * values, axis=1, keepdims=True)
        sums[...] = jnp.zeros_like(sums)
        totals[...] = jnp.zeros_like(totals)

    rows = dot(product[...], upper[...], (1, 0), HIGHEST).astype(BF)
    panel[...] = rows
    values = rows.astype(F32)
    length = jnp.sqrt(jnp.sum(values * values, axis=1, keepdims=True) + EPS)
    points = (values / length).astype(BF)
    scores = (2.0 * unit) * dot(centroids[...], points, (1, 1)) - norms[...]
    shifted = jnp.exp2(scores - jnp.max(scores, axis=0, keepdims=True))
    resp = (shifted * (1.0 / jnp.sum(shifted, axis=0, keepdims=True))).astype(BF)
    sums[...] += dot(resp, points, (1, 0))
    totals[...] += dot(jnp.ones((8, resp.shape[1]), BF), resp, (1, 1))

    @pl.when(step == pl.num_programs(0) - 1)
    def _():
        share = sums.shape[0] // packed.shape[0]
        lanes = sums.shape[1]
        count = share // lanes
        for piece in range(packed.shape[0]):
            at = piece * share
            packed[piece, :share, :] = sums[at : at + share, :].astype(BF)
            mass = jnp.concatenate(
                [totals[0:1, at + k * lanes : at + (k + 1) * lanes] for k in range(count)], axis=0
            )
            high = mass.astype(BF).astype(F32)
            blank = jnp.zeros((16 - 2 * count, lanes), F32)
            tail = jnp.concatenate([high, mass - high, blank], axis=0)
            packed[piece, share:, :] = tail.astype(BF)


def cluster(product, upper, centroids, pieces, chunk):
    rows, rank = product.shape
    count = centroids.shape[0]
    parcel = (pieces, count // pieces + 16, rank)
    return pl.pallas_call(
        cluster_body,
        grid=(rows // chunk,),
        in_specs=[
            pl.BlockSpec((chunk, rank), lambda i: (i, 0)),
            whole(upper.shape),
            whole(centroids.shape),
        ],
        out_specs=[pl.BlockSpec((chunk, rank), lambda i: (i, 0)), whole(parcel)],
        out_shape=[jax.ShapeDtypeStruct((rows, rank), BF), jax.ShapeDtypeStruct(parcel, BF)],
        scratch_shapes=[
            pltpu.VMEM((count, rank), F32),
            pltpu.VMEM((8, count), F32),
            pltpu.VMEM((count, 1), F32),
        ],
        name="cluster",
    )(product, upper, centroids)


def gathered_sum_body(parts, out):
    out[...] = jnp.sum(parts[...].astype(F32), axis=0)


def centers_body(where, first, second, third, fourth, centroids, out):
    at = where[0]
    parts = (first, second, third, fourth)
    stack = [part[...] for part in parts]
    total = jnp.zeros_like(stack[0])
    for y in range(SIDE):
        place = (at + SIDE - y) % SIDE
        pick = stack[0]
        for k in range(1, SIDE):
            pick = jnp.where(place == k, stack[k], pick)
        total = total + pick
    share = out.shape[0]
    lanes = out.shape[1]
    mass = total[share : share + share // lanes] + total[share + share // lanes : share + 2 * (share // lanes)]
    for k in range(share // lanes):
        column = jnp.transpose(jnp.broadcast_to(mass[k : k + 1], (lanes, lanes)))
        block = slice(k * lanes, (k + 1) * lanes)
        out[block, :] = (
            (total[block] + centroids[block].astype(F32)) / (column + 1.0)
        ).astype(BF)


def shards(tiles, tile_list, tile_count, scale_index, scales, panel_start, centroids):
    block_size = tiles.shape[1]
    piece, rank = panel_start.shape
    rows_axis = lax.axis_size("row")
    cols_axis = lax.axis_size("col")
    total_rows = piece * rows_axis * cols_axis
    row_at = lax.axis_index("row")
    col_at = lax.axis_index("col")
    row_blocks = piece * cols_axis // block_size
    col_blocks = piece * rows_axis // block_size
    meta = jnp.concatenate(
        [
            tile_list[:, 0] - row_at * row_blocks,
            tile_list[:, 1] - col_at * col_blocks,
            tile_count,
            jnp.stack([col_at // 2, col_at % 2]).astype(jnp.int32),
        ]
    )
    where = (col_at // 2).astype(jnp.int32)[None]
    table_ids = jnp.arange(scales.shape[0], dtype=jnp.int32)
    weights = jnp.sum(
        jnp.where(scale_index[:, None] == table_ids[None, :], scales[None, :], 0.0), axis=1
    )
    square = jax.ShapeDtypeStruct((rank, rank), F32)
    tall = jax.ShapeDtypeStruct((piece, rank), BF)
    tall_f32 = jax.ShapeDtypeStruct((piece, rank), F32)
    smem = pl.BlockSpec(memory_space=pltpu.SMEM)
    vmem = pl.BlockSpec(memory_space=pltpu.VMEM)

    copies_shape = jax.ShapeDtypeStruct((rows_axis, rank, piece), BF)
    panel = panel_start
    gram = None
    for round_index in range(ROUNDS):
        mine = jnp.stack([panel] + [shift_col(panel, d, 0) for d in (1, 2, 3)])
        theirs = shift_col(mine, 0, 1)
        if gram is not None:
            theirs, gram = lax.optimization_barrier((theirs, sum_x(gram)))
            gram = sum_z(gram)
        (partial,) = tile_call(
            down_body, "down", meta, weights, [mine, theirs], tiles,
            [jax.ShapeDtypeStruct((rows_axis, rank, piece), BF)],
            [pltpu.VMEM((col_blocks, rank, block_size), F32), pltpu.VMEM((block_size, rank), BF)],
        )
        if gram is None:
            parts = lax.all_to_all(partial, "row", 0, 0, tiled=True)
            copies, gram = small_call(
                reduce_first_body, "reduce_first", [copies_shape, square], parts
            )
        else:
            partial, gram = lax.optimization_barrier((partial, gram))
            parts = lax.all_to_all(partial, "row", 0, 0, tiled=True)
            gram = sum_y(gram)
            upper = factor_of(total_rows, gram, shift_col(gram, 0, 1))
            copies, gram = small_call(
                reduce_down_body, "reduce_down", [copies_shape, square], parts, upper
            )
        gathered = lax.all_to_all(copies, "row", 0, 0, tiled=True)
        gram = sum_y(gram)
        gram = sum_x(gram + shift_col(gram, 0, 1))
        gathered, gram = lax.optimization_barrier((gathered, gram))
        gram = sum_z(gram)
        keep, send = tile_call(
            up_body, "up", meta, weights, [gathered], tiles,
            [jax.ShapeDtypeStruct((SIDE, piece, rank), F32)] * 2,
            [pltpu.VMEM((row_blocks, block_size, rank), F32)],
        )
        got = shift_col(send, 0, 1)
        own, one, two, three = pl.pallas_call(
            fold_body,
            in_specs=[smem, vmem, vmem],
            out_shape=[tall_f32, tall, tall, tall],
            name="fold",
        )(where, keep, got)
        gram, own = lax.optimization_barrier((gram, own))
        upper = factor_of(total_rows, gram)
        one, two, three = shift_col(one, 1, 0), shift_col(two, 2, 0), shift_col(three, 3, 0)
        last = round_index + 1 == ROUNDS
        panel, gram = small_call(
            reduce_last_body if last else reduce_up_body,
            "reduce_last" if last else "reduce_up",
            [tall_f32 if last else tall, square], own, one, two, three, upper,
        )
    gram = sum_y(sum_z(sum_x(gram)))
    upper = factor_of(total_rows, gram, shift_col(gram, 0, 1))

    count = centroids.shape[0]
    share = count // rows_axis
    panel, packed = cluster(panel, upper, centroids, rows_axis, 256)
    parts = lax.all_to_all(packed, "row", 0, 0, tiled=True)
    mass = small_call(
        gathered_sum_body, "mass", jax.ShapeDtypeStruct((share + 16, rank), F32), parts
    )
    mass = mass + shift_col(mass, 0, 1)
    owned = lax.dynamic_slice_in_dim(centroids, row_at * share, share, 0)
    centers = pl.pallas_call(
        centers_body,
        in_specs=[smem] + [vmem] * 5,
        out_shape=jax.ShapeDtypeStruct((share, rank), BF),
        name="centers",
    )(where, mass, shift_col(mass, 1, 0), shift_col(mass, 2, 0), shift_col(mass, 3, 0), owned)
    copies = jnp.broadcast_to(centers[None], (rows_axis,) + centers.shape)
    centers = lax.all_to_all(copies, "row", 0, 0, tiled=True)
    return (panel, centers.reshape(count, rank).astype(F32))


def solution(mesh):
    return jax.shard_map(
        shards,
        mesh=mesh,
        in_specs=(
            P(("row", "col"), None, None),
            P(("row", "col"), None),
            P(("row", "col")),
            P(("row", "col")),
            P(),
            P(("row", "col"), None),
            P(),
        ),
        out_specs=(P(("row", "col"), None), P()),
        check_vma=False,
    )
```

```python
import functools
import math

import jax
import jax.numpy as jnp
from jax import lax
from jax.experimental import pallas as pl
from jax.experimental.pallas import tpu as pltpu
from jax.sharding import PartitionSpec as P

ROUNDS = 2
SHARPNESS = 48.0
EPS = 1e-06
CLOSE = 1e-05

SIDE = 4
BF = jnp.bfloat16
F32 = jnp.float32
HIGHEST = lax.Precision.HIGHEST


def dot(a, b, contract, precision=None):
    return lax.dot_general(
        a, b, ((contract[:1], contract[1:]), ((), ())), precision=precision,
        preferred_element_type=F32,
    )


def shift_row(value, dx, dz):
    pairs = [
        (x * SIDE + z, (x + dx) % SIDE * SIDE + (z + dz) % SIDE)
        for x in range(SIDE)
        for z in range(SIDE)
    ]
    return lax.ppermute(value, "row", pairs)


def shift_col(value, dy, dc):
    pairs = [
        (y * 2 + c, (y + dy) % SIDE * 2 + (c + dc) % 2) for y in range(SIDE) for c in range(2)
    ]
    return lax.ppermute(value, "col", pairs)


def near(value):
    return pltpu.with_memory_space_constraint(value, pltpu.VMEM)


def small_call(body, out_shapes, *args, where=None, scratch=(), far=0):
    scalars = [] if where is None else [where]
    return pl.pallas_call(
        body,
        in_specs=[pl.BlockSpec(memory_space=pltpu.SMEM)] * len(scalars)
        + [pl.BlockSpec(memory_space=pltpu.VMEM)] * len(args),
        out_shape=out_shapes,
        scratch_shapes=scratch,
    )(*scalars, *args[:far], *(near(arg) for arg in args[far:]))


def each_tile(meta, tiles, buffers, arrivals, acc, add):
    def load(slot):
        return pltpu.make_async_copy(tiles.at[slot], buffers.at[slot], arrivals.at[slot])

    def start(slot, carry):
        load(slot).start()
        return carry

    def finish(slot, carry):
        load(slot).wait()
        add(slot)
        return carry

    lax.fori_loop(0, meta[12], start, 0)
    acc[...] = jnp.zeros_like(acc)
    lax.fori_loop(0, meta[12], finish, 0)


def down_body(meta, weights, mine, theirs, tiles, out, acc, rows, buffers, arrivals):
    half = mine.shape[1]
    core = meta[14]

    def add(slot):
        place = (meta[13] + SIDE - meta[slot]) % SIDE
        rows[pl.ds(pl.multiple_of(core * half, half), half), :] = mine[place]
        rows[pl.ds(pl.multiple_of((1 - core) * half, half), half), :] = theirs[place]
        product = dot(rows[...], buffers[slot], (0, 0))
        target = meta[6 + slot]
        acc[target] = acc[target] + weights[slot] * product

    each_tile(meta, tiles, buffers, arrivals, acc, add)
    for block in range(acc.shape[0]):
        out[2 * block] = acc[block, :, :half].astype(BF)
        out[2 * block + 1] = acc[block, :, half:].astype(BF)


def up_body(meta, weights, gathered, tiles, keep, send, acc, buffers, arrivals):
    half = gathered.shape[2]
    core = meta[14]

    def add(slot):
        source = meta[6 + slot]
        product = dot(buffers[slot, :, :half], gathered[2 * source], (1, 1))
        product += dot(buffers[slot, :, half:], gathered[2 * source + 1], (1, 1))
        target = meta[slot]
        acc[target] = acc[target] + weights[slot] * product

    each_tile(meta, tiles, buffers, arrivals, acc, add)
    for block in range(acc.shape[0]):
        keep[block] = acc[block, pl.ds(pl.multiple_of(core * half, half), half), :]
        send[block] = acc[block, pl.ds(pl.multiple_of((1 - core) * half, half), half), :]


def tile_call(body, meta, weights, panels, tiles, outs, scratch):
    slots, block, _ = tiles.shape
    return pl.pallas_call(
        body,
        in_specs=[pl.BlockSpec(memory_space=pltpu.SMEM)] * 2
        + [pl.BlockSpec(memory_space=pltpu.VMEM)] * len(panels)
        + [pl.BlockSpec(memory_space=pl.ANY)],
        out_shape=outs,
        scratch_shapes=scratch
        + [pltpu.VMEM(tiles.shape, BF), pltpu.SemaphoreType.DMA((slots,))],
        cost_estimate=pl.CostEstimate(
            flops=2 * slots * block * block * 128,
            transcendentals=0,
            bytes_accessed=slots * block * block * 2 + 4 * 1024 * 1024,
        ),
    )(meta, weights, *(near(panel) for panel in panels), tiles)


def share_wide(total, out, gram):
    factor = total.astype(BF)
    for copy in range(out.shape[0]):
        out[copy] = factor
    gram[...] = dot(factor, factor, (1, 1))


def reduce_first_body(parts, out, gram):
    share_wide(jnp.sum(parts[...].astype(F32), axis=0), out, gram)


def reduce_down_body(parts, upper, out, gram):
    total = jnp.sum(parts[...].astype(F32), axis=0)
    share_wide(dot(upper[...], total, (0, 0), HIGHEST), out, gram)


def fold_body(where, keep, got, own, one, two, three):
    at = where[0]
    own[...] = keep[at] + got[at]
    for distance, out in ((1, one), (2, two), (3, three)):
        to = (at + distance) % SIDE
        out[...] = (keep[to] + got[to]).astype(BF)


def reduce_up_body(own, one, two, three, upper, out, gram):
    total = own[...] + one[...].astype(F32) + two[...].astype(F32) + three[...].astype(F32)
    panel = dot(total, upper[...], (1, 0), HIGHEST).astype(BF)
    out[...] = panel
    gram[...] = dot(panel, panel, (0, 0))


def reduce_last_body(own, one, two, three, upper, out, gram):
    total = own[...] + one[...].astype(F32) + two[...].astype(F32) + three[...].astype(F32)
    total = dot(total, upper[...], (1, 0), HIGHEST)
    out[...] = total
    gram[...] = dot(total, total, (0, 0), HIGHEST)


def factor_body(total_rows, *refs):
    *grams, out, work, build = refs
    gram = sum(part[...] for part in grams) / total_rows
    size = gram.shape[0]
    down = lax.broadcasted_iota(jnp.int32, (size, size), 0)
    across = lax.broadcasted_iota(jnp.int32, (size, size), 1)
    eye = jnp.where(down == across, 1.0, 0.0).astype(F32)
    keep = jnp.where(down < across, 1.0, 0.5 * eye)
    diagonal = gram * eye
    tall = lax.rsqrt(jnp.sum(diagonal, axis=1, keepdims=True))
    scaled = gram * tall * lax.rsqrt(jnp.sum(diagonal, axis=0, keepdims=True))
    build[...] = eye - keep * (scaled - eye)

    def refine(state):
        at, _ = state
        guess = build[...]
        excess = dot(guess, dot(scaled, guess, (1, 0), HIGHEST), (0, 0), HIGHEST) - eye
        build[...] = guess - dot(guess, keep * excess, (1, 0), HIGHEST)
        return at + 1, jnp.max(jnp.abs(excess))

    def unfinished(state):
        at, error = state
        return (at < 10) & jnp.logical_not(error < CLOSE)

    _, error = lax.while_loop(unfinished, refine, (jnp.int32(0), jnp.float32(1.0)))
    out[...] = build[...] * tall

    @pl.when(jnp.logical_not(error < CLOSE))
    def _():
        work[...] = gram
        build[...] = eye

        def eliminate(k, carry):
            row = work[pl.ds(k, 1), :]
            pivot = jnp.sum(jnp.where(across[:1] == k, row, 0.0), axis=1, keepdims=True)
            column = jnp.sum(jnp.where(across == k, work[...], 0.0), axis=1, keepdims=True)
            ratio = jnp.where(down[:, :1] > k, column / pivot, 0.0)
            unit = build[pl.ds(k, 1), :]
            work[...] = work[...] - ratio * row
            build[...] = build[...] - ratio * unit
            return carry

        lax.fori_loop(0, size, eliminate, 0)
        pivots = jnp.sum(work[...] * eye, axis=1, keepdims=True)
        out[...] = jnp.transpose(build[...] * lax.rsqrt(pivots))


def ring(value, shift):
    return [value] + [shift(value, d) for d in (1, 2, 3)]


def ring_sum(value, shift):
    return sum(ring(value, shift))


def sum_x(value):
    return ring_sum(value, lambda v, d: shift_row(v, d, 0))


def sum_z(value):
    return ring_sum(value, lambda v, d: shift_row(v, 0, d))


def sum_y(value):
    return ring_sum(value, lambda v, d: shift_col(v, d, 0))


def factor_of(total_rows, *grams):
    gram = grams[0]
    return small_call(
        functools.partial(factor_body, total_rows),
        pltpu.VMEM(gram.shape, F32), *grams,
        scratch=[pltpu.VMEM(gram.shape, F32)] * 2,
    )


def cluster_body(where, product, upper, centroids, panel, keep, send, sums, totals, norms):
    step = pl.program_id(0)
    unit = SHARPNESS * math.log2(math.e)
    lanes = sums.shape[1]

    @pl.when(step == 0)
    def _():
        values = centroids[...].astype(F32)
        norms[...] = unit * jnp.sum(values * values, axis=1, keepdims=True)
        sums[...] = jnp.zeros_like(sums)
        totals[...] = jnp.zeros_like(totals)

    rows = dot(product[...], upper[...], (1, 0), HIGHEST).astype(BF)
    panel[...] = rows
    values = rows.astype(F32)
    length = jnp.sqrt(jnp.sum(values * values, axis=1, keepdims=True) + EPS)
    points = (values / length).astype(BF)
    scores = (2.0 * unit) * dot(centroids[...], points, (1, 1)) - norms[...]
    shifted = jnp.exp2(scores - jnp.max(scores, axis=0, keepdims=True))
    resp = (shifted * (1.0 / jnp.sum(shifted, axis=0, keepdims=True))).astype(BF)
    sums[...] += dot(resp, points, (1, 0))
    ones = jnp.ones((8, resp.shape[1]), BF)
    for block in range(totals.shape[0]):
        totals[block] += dot(ones, resp[block * lanes : (block + 1) * lanes], (1, 1))

    @pl.when(step == pl.num_programs(0) - 1)
    def _():
        core = where[1]
        blank = jnp.zeros((14, lanes), F32)
        for piece in range(keep.shape[0]):
            block = core * keep.shape[0] + piece
            keep[piece, :lanes, :] = sums[pl.ds(pl.multiple_of(block * lanes, lanes), lanes), :]
            keep[piece, lanes:, :] = jnp.concatenate(
                [totals[block, 0:1], jnp.zeros((1, lanes), F32), blank], axis=0
            )
            block = (1 - core) * keep.shape[0] + piece
            out = sums[pl.ds(pl.multiple_of(block * lanes, lanes), lanes), :]
            send[piece, :lanes, :] = out.astype(BF)
            send[piece, lanes:, :] = pair(totals[block, 0:1]).astype(BF)


def pair(mass):
    high = mass.astype(BF).astype(F32)
    return jnp.concatenate([high, mass - high, jnp.zeros((14, mass.shape[1]), F32)], axis=0)


def cluster(where, product, upper, centroids, pieces, chunk):
    rows, rank = product.shape
    count = centroids.shape[0]
    parcel = (pieces, rank + 16, rank)
    return pl.pallas_call(
        cluster_body,
        grid=(rows // chunk,),
        in_specs=[
            pl.BlockSpec(memory_space=pltpu.SMEM),
            pl.BlockSpec((chunk, rank), lambda i: (i, 0)),
            pl.BlockSpec(memory_space=pltpu.VMEM),
            pl.BlockSpec((count, rank), lambda i: (0, 0)),
        ],
        out_specs=[
            pl.BlockSpec((chunk, rank), lambda i: (i, 0)),
            pl.BlockSpec(parcel, lambda i: (0, 0, 0)),
            pl.BlockSpec(parcel, lambda i: (0, 0, 0)),
        ],
        out_shape=[
            jax.ShapeDtypeStruct((rows, rank), BF),
            jax.ShapeDtypeStruct(parcel, F32),
            jax.ShapeDtypeStruct(parcel, BF),
        ],
        scratch_shapes=[
            pltpu.VMEM((count, rank), F32),
            pltpu.VMEM((count // rank, 8, rank), F32),
            pltpu.VMEM((count, 1), F32),
        ],
        name="cluster",
    )(where, product, near(upper), centroids)


def pool_body(keep, got, out):
    lanes = out.shape[2]
    out[:, :lanes, :] = (keep[:, :lanes, :] + got[:, :lanes, :].astype(F32)).astype(BF)
    for piece in range(out.shape[0]):
        tail = got[piece, lanes:, :].astype(F32)
        mass = keep[piece, lanes : lanes + 1, :] + tail[0:1] + tail[1:2]
        out[piece, lanes:, :] = pair(mass).astype(BF)


def mass_body(parts, out):
    lanes = out.shape[1]
    total = jnp.sum(parts[...].astype(F32), axis=0)
    out[:lanes, :] = total[:lanes]
    out[lanes:, :] = jnp.broadcast_to(total[lanes : lanes + 1] + total[lanes + 1 : lanes + 2], (8, lanes))


def centers_body(where, first, second, third, fourth, centroids, out):
    stack = [part[...] for part in (first, second, third, fourth)]
    lanes = out.shape[2]
    total = jnp.zeros_like(stack[0])
    for y in range(SIDE):
        place = (where[0] + SIDE - y) % SIDE
        pick = stack[0]
        for k in range(1, SIDE):
            pick = jnp.where(place == k, stack[k], pick)
        total = total + pick
    column = jnp.transpose(jnp.broadcast_to(total[lanes : lanes + 1], (lanes, lanes)))
    values = ((total[:lanes] + centroids[...].astype(F32)) / (column + 1.0)).astype(BF)
    for copy in range(out.shape[0]):
        out[copy] = values


def centers_of(where, masses, centroids, pieces):
    lanes = centroids.shape[1]
    near_spec = pl.BlockSpec(memory_space=pltpu.VMEM)
    return pl.pallas_call(
        centers_body,
        grid_spec=pltpu.PrefetchScalarGridSpec(
            num_scalar_prefetch=1,
            grid=(1,),
            in_specs=[near_spec] * len(masses)
            + [pl.BlockSpec((lanes, lanes), lambda i, at: (at[1] * pieces + at[2], 0))],
            out_specs=pl.BlockSpec((pieces, lanes, lanes), lambda i, at: (0, 0, 0)),
        ),
        out_shape=jax.ShapeDtypeStruct((pieces, lanes, lanes), BF),
        name="centers",
    )(where, *(near(mass) for mass in masses), centroids)


def join_body(where, mine, theirs, out):
    core = where[1]
    lanes = out.shape[2]
    for piece in range(mine.shape[0]):
        rows = slice(piece * lanes, (piece + 1) * lanes)
        out[core, rows, :] = mine[piece].astype(F32)
        out[1 - core, rows, :] = theirs[piece].astype(F32)


def shards(tiles, tile_list, tile_count, scale_index, scales, panel_start, centroids):
    block_size = tiles.shape[1]
    piece, rank = panel_start.shape
    rows_axis = lax.axis_size("row")
    cols_axis = lax.axis_size("col")
    total_rows = piece * rows_axis * cols_axis
    row_at = lax.axis_index("row")
    col_at = lax.axis_index("col")
    row_blocks = piece * cols_axis // block_size
    col_blocks = piece * rows_axis // block_size
    meta = jnp.concatenate(
        [
            tile_list[:, 0] - row_at * row_blocks,
            tile_list[:, 1] - col_at * col_blocks,
            tile_count,
            jnp.stack([col_at // 2, col_at % 2]).astype(jnp.int32),
        ]
    )
    where = jnp.stack([col_at // 2, col_at % 2, row_at]).astype(jnp.int32)
    table_ids = jnp.arange(scales.shape[0], dtype=jnp.int32)
    weights = jnp.sum(
        jnp.where(scale_index[:, None] == table_ids[None, :], scales[None, :], 0.0), axis=1
    )
    spot = pltpu.VMEM
    square = spot((rank, rank), F32)
    tall = spot((piece, rank), BF)
    tall_f32 = spot((piece, rank), F32)

    copies_shape = jax.ShapeDtypeStruct((rows_axis, rank, piece), BF)
    panel = panel_start
    gram = None
    for round_index in range(ROUNDS):
        last = round_index + 1 == ROUNDS
        shifted = [shift_col(panel, d, 0) for d in (1, 2, 3)]
        if gram is not None:
            *shifted, gram = lax.optimization_barrier((*shifted, sum_x(gram)))
            gram = sum_z(gram)
        mine = jnp.stack([panel] + shifted)
        theirs = shift_col(mine, 0, 1)
        partial = tile_call(
            down_body, meta, weights, [mine, theirs], tiles, copies_shape,
            [pltpu.VMEM((col_blocks, rank, block_size), F32), pltpu.VMEM((block_size, rank), BF)],
        )
        if gram is None:
            parts = lax.all_to_all(partial, "row", 0, 0, tiled=True)
            copies, gram = small_call(reduce_first_body, [copies_shape, square], parts)
        else:
            partial, gram = lax.optimization_barrier((partial, gram))
            parts = lax.all_to_all(partial, "row", 0, 0, tiled=True)
            gram = sum_y(gram)
            upper = factor_of(total_rows, gram, shift_col(gram, 0, 1))
            copies, gram = small_call(reduce_down_body, [copies_shape, square], parts, upper)
        gathered = lax.all_to_all(copies, "row", 0, 0, tiled=True)
        gram = sum_y(gram)
        gram = sum_x(gram + shift_col(gram, 0, 1))
        gathered, gram = lax.optimization_barrier((gathered, gram))
        grams = ring(gram, lambda v, d: shift_row(v, 0, d))
        keep, send = tile_call(
            up_body, meta, weights, [gathered], tiles,
            [jax.ShapeDtypeStruct((SIDE, piece, rank), F32)] * 2,
            [pltpu.VMEM((row_blocks, block_size, rank), F32)],
        )
        got = shift_col(send, 0, 1)
        own, one, two, three = small_call(
            fold_body, [tall_f32, tall, tall, tall], keep, got, where=where,
            far=1,
        )
        *grams, own = lax.optimization_barrier((*grams, own))
        upper = factor_of(total_rows, *grams)
        one, two, three = shift_col(one, 1, 0), shift_col(two, 2, 0), shift_col(three, 3, 0)
        panel, gram = small_call(
            reduce_last_body if last else reduce_up_body,
            [tall_f32 if last else tall, square], own, one, two, three, upper,
        )
    gram = sum_y(gram + shift_col(gram, 0, 1))
    upper = factor_of(total_rows, *ring(sum_x(gram), lambda v, d: shift_row(v, 0, d)))

    panel, keep, send = cluster(where, panel, upper, centroids, rows_axis, 256)
    got = shift_col(send, 0, 1)
    packed = small_call(pool_body, spot(send.shape, BF), keep, got, far=1)
    parts = lax.all_to_all(packed, "row", 0, 0, tiled=True)
    mass = small_call(mass_body, spot((rank + 8, rank), F32), parts)
    masses = [mass] + [shift_col(mass, d, 0) for d in (1, 2, 3)]
    copies = centers_of(where, masses, centroids, rows_axis)
    mine = lax.all_to_all(copies, "row", 0, 0, tiled=True)
    theirs = shift_col(mine, 0, 1)
    count = centroids.shape[0]
    centers = small_call(
        join_body, jax.ShapeDtypeStruct((2, count // 2, rank), F32), mine, theirs,
        where=where,
    )
    return (panel, centers.reshape(count, rank))


def solution(mesh):
    return jax.shard_map(
        shards,
        mesh=mesh,
        in_specs=(
            P(("row", "col"), None, None),
            P(("row", "col"), None),
            P(("row", "col")),
            P(("row", "col")),
            P(),
            P(("row", "col"), None),
            P(),
        ),
        out_specs=(P(("row", "col"), None), P()),
        check_vma=False,
    )
```

```python
import functools
import math

import jax
import jax.numpy as jnp
from jax import lax
from jax.experimental import pallas as pl
from jax.experimental.pallas import tpu as pltpu
from jax.sharding import PartitionSpec as P

ROUNDS = 2
SHARPNESS = 48.0
EPS = 1e-06
CLOSE = 1e-05
CHUNK = 512

SIDE = 4
BF = jnp.bfloat16
F32 = jnp.float32
HIGHEST = lax.Precision.HIGHEST


def dot(a, b, contract, precision=None):
    return lax.dot_general(
        a, b, ((contract[:1], contract[1:]), ((), ())), precision=precision,
        preferred_element_type=F32,
    )


def shift_row(value, dx, dz):
    pairs = [
        (x * SIDE + z, (x + dx) % SIDE * SIDE + (z + dz) % SIDE)
        for x in range(SIDE)
        for z in range(SIDE)
    ]
    return lax.ppermute(value, "row", pairs)


def shift_col(value, dy, dc):
    pairs = [
        (y * 2 + c, (y + dy) % SIDE * 2 + (c + dc) % 2) for y in range(SIDE) for c in range(2)
    ]
    return lax.ppermute(value, "col", pairs)


def near(value):
    return pltpu.with_memory_space_constraint(value, pltpu.VMEM)


def small_call(body, out_shapes, *args, where=None, scratch=(), far=0):
    scalars = [] if where is None else [where]
    return pl.pallas_call(
        body,
        in_specs=[pl.BlockSpec(memory_space=pltpu.SMEM)] * len(scalars)
        + [pl.BlockSpec(memory_space=pltpu.VMEM)] * len(args),
        out_shape=out_shapes,
        scratch_shapes=scratch,
    )(*scalars, *args[:far], *(near(arg) for arg in args[far:]))


def each_tile(meta, tiles, buffers, arrivals, acc, add):
    def load(slot):
        return pltpu.make_async_copy(tiles.at[slot], buffers.at[slot], arrivals.at[slot])

    def start(slot, carry):
        load(slot).start()
        return carry

    def finish(slot, carry):
        load(slot).wait()
        add(slot)
        return carry

    lax.fori_loop(0, meta[12], start, 0)
    acc[...] = jnp.zeros_like(acc)
    lax.fori_loop(0, meta[12], finish, 0)


def down_body(meta, weights, mine, theirs, tiles, out, acc, rows, buffers, arrivals):
    half = mine.shape[1]
    core = meta[14]

    def add(slot):
        place = (meta[13] + SIDE - meta[slot]) % SIDE
        rows[pl.ds(pl.multiple_of(core * half, half), half), :] = mine[place]
        rows[pl.ds(pl.multiple_of((1 - core) * half, half), half), :] = theirs[place]
        product = dot(rows[...], buffers[slot], (0, 0))
        target = meta[6 + slot]
        acc[target] = acc[target] + weights[slot] * product

    each_tile(meta, tiles, buffers, arrivals, acc, add)
    for block in range(acc.shape[0]):
        out[2 * block] = acc[block, :, :half].astype(BF)
        out[2 * block + 1] = acc[block, :, half:].astype(BF)


def up_body(meta, weights, gathered, tiles, keep, send, acc, buffers, arrivals):
    half = gathered.shape[2]
    core = meta[14]

    def add(slot):
        source = meta[6 + slot]
        product = dot(buffers[slot, :, :half], gathered[2 * source], (1, 1))
        product += dot(buffers[slot, :, half:], gathered[2 * source + 1], (1, 1))
        target = meta[slot]
        acc[target] = acc[target] + weights[slot] * product

    each_tile(meta, tiles, buffers, arrivals, acc, add)
    for block in range(acc.shape[0]):
        keep[block] = acc[block, pl.ds(pl.multiple_of(core * half, half), half), :]
        send[block] = acc[block, pl.ds(pl.multiple_of((1 - core) * half, half), half), :]


def tile_call(body, meta, weights, panels, tiles, outs, scratch):
    slots, block, _ = tiles.shape
    return pl.pallas_call(
        body,
        in_specs=[pl.BlockSpec(memory_space=pltpu.SMEM)] * 2
        + [pl.BlockSpec(memory_space=pltpu.VMEM)] * len(panels)
        + [pl.BlockSpec(memory_space=pl.ANY)],
        out_shape=outs,
        scratch_shapes=scratch
        + [pltpu.VMEM(tiles.shape, BF), pltpu.SemaphoreType.DMA((slots,))],
        cost_estimate=pl.CostEstimate(
            flops=2 * slots * block * block * 128,
            transcendentals=0,
            bytes_accessed=slots * block * block * 2 + 4 * 1024 * 1024,
        ),
    )(meta, weights, *(near(panel) for panel in panels), tiles)


def share_wide(total, out, gram):
    factor = total.astype(BF)
    for copy in range(out.shape[0]):
        out[copy] = factor
    gram[...] = dot(factor, factor, (1, 1))


def reduce_first_body(parts, out, gram):
    share_wide(jnp.sum(parts[...].astype(F32), axis=0), out, gram)


def reduce_down_body(parts, upper, out, gram):
    total = jnp.sum(parts[...].astype(F32), axis=0)
    share_wide(dot(upper[...], total, (0, 0), HIGHEST), out, gram)


def fold_body(where, keep, got, own, one, two, three):
    at = where[0]
    own[...] = keep[at] + got[at]
    for distance, out in ((1, one), (2, two), (3, three)):
        to = (at + distance) % SIDE
        out[...] = (keep[to] + got[to]).astype(BF)


def reduce_up_body(own, one, two, three, upper, out, gram):
    total = own[...] + one[...].astype(F32) + two[...].astype(F32) + three[...].astype(F32)
    panel = dot(total, upper[...], (1, 0), HIGHEST).astype(BF)
    out[...] = panel
    gram[...] = dot(panel, panel, (0, 0))


def reduce_last_body(own, one, two, three, upper, out, gram):
    total = own[...] + one[...].astype(F32) + two[...].astype(F32) + three[...].astype(F32)
    total = dot(total, upper[...], (1, 0), HIGHEST)
    out[...] = total
    gram[...] = dot(total, total, (0, 0), HIGHEST)


def factor_body(total_rows, *refs):
    *grams, out, work, build = refs
    gram = sum(part[...] for part in grams) / total_rows
    size = gram.shape[0]
    down = lax.broadcasted_iota(jnp.int32, (size, size), 0)
    across = lax.broadcasted_iota(jnp.int32, (size, size), 1)
    eye = jnp.where(down == across, 1.0, 0.0).astype(F32)
    keep = jnp.where(down < across, 1.0, 0.5 * eye)
    diagonal = gram * eye
    tall = lax.rsqrt(jnp.sum(diagonal, axis=1, keepdims=True))
    scaled = gram * tall * lax.rsqrt(jnp.sum(diagonal, axis=0, keepdims=True))
    build[...] = eye - keep * (scaled - eye)

    def refine(state):
        at, _ = state
        guess = build[...]
        excess = dot(guess, dot(scaled, guess, (1, 0), HIGHEST), (0, 0), HIGHEST) - eye
        build[...] = guess - dot(guess, keep * excess, (1, 0), HIGHEST)
        return at + 1, jnp.max(jnp.abs(excess))

    def unfinished(state):
        at, error = state
        return (at < 10) & jnp.logical_not(error < CLOSE)

    _, error = lax.while_loop(unfinished, refine, (jnp.int32(0), jnp.float32(1.0)))
    out[...] = build[...] * tall

    @pl.when(jnp.logical_not(error < CLOSE))
    def _():
        work[...] = gram
        build[...] = eye

        def eliminate(k, carry):
            row = work[pl.ds(k, 1), :]
            pivot = jnp.sum(jnp.where(across[:1] == k, row, 0.0), axis=1, keepdims=True)
            column = jnp.sum(jnp.where(across == k, work[...], 0.0), axis=1, keepdims=True)
            ratio = jnp.where(down[:, :1] > k, column / pivot, 0.0)
            unit = build[pl.ds(k, 1), :]
            work[...] = work[...] - ratio * row
            build[...] = build[...] - ratio * unit
            return carry

        lax.fori_loop(0, size, eliminate, 0)
        pivots = jnp.sum(work[...] * eye, axis=1, keepdims=True)
        out[...] = jnp.transpose(build[...] * lax.rsqrt(pivots))


def ring(value, shift):
    return [value] + [shift(value, d) for d in (1, 2, 3)]


def ring_sum(value, shift):
    return sum(ring(value, shift))


def sum_x(value):
    return ring_sum(value, lambda v, d: shift_row(v, d, 0))


def sum_z(value):
    return ring_sum(value, lambda v, d: shift_row(v, 0, d))


def sum_y(value):
    return ring_sum(value, lambda v, d: shift_col(v, d, 0))


def factor_of(total_rows, *grams):
    gram = grams[0]
    return small_call(
        functools.partial(factor_body, total_rows),
        pltpu.VMEM(gram.shape, F32), *grams,
        scratch=[pltpu.VMEM(gram.shape, F32)] * 2,
    )


def widen_body(centroids, out):
    count, lanes = centroids.shape
    values = centroids[...].astype(F32)
    norms = -0.5 * jnp.sum(values * values, axis=1, keepdims=True)
    high = norms.astype(BF).astype(F32)
    middle = (norms - high).astype(BF).astype(F32)
    lane = lax.broadcasted_iota(jnp.int32, (count, lanes), 1)
    parts = jnp.where(lane == 2, norms - high - middle, 0.0)
    parts = jnp.where(lane == 1, middle, parts)
    out[:, :lanes] = centroids[...]
    out[:, lanes:] = jnp.where(lane == 0, high, parts).astype(BF)


def cluster_body(where, product, upper, source, panel, keep, send, sums, totals, buffer, wide, arrival):
    load = pltpu.make_async_copy(source, wide, arrival)
    load.start()
    twice = 2.0 * SHARPNESS * math.log2(math.e)
    count, lanes = sums.shape
    blocks = count // CHUNK
    rows = dot(product[...], upper[...], (1, 0), HIGHEST).astype(BF)
    panel[...] = rows
    values = rows.astype(F32)
    length = jnp.sqrt(jnp.sum(values * values, axis=1, keepdims=True) + EPS)
    points = (values / length).astype(BF)
    size = points.shape[0]
    lane = lax.broadcasted_iota(jnp.int32, points.shape, 1)
    wide_points = jnp.concatenate([points, jnp.where(lane < 3, 1.0, 0.0).astype(BF)], axis=1)
    load.wait()

    top = None
    for block in range(blocks):
        at = slice(block * CHUNK, (block + 1) * CHUNK)
        scores = dot(wide[at], wide_points, (1, 1))
        buffer[at] = scores
        most = jnp.max(scores.reshape(CHUNK // 8, 8, size), axis=0)
        top = most if top is None else jnp.maximum(top, most)
    top = twice * jnp.max(top, axis=0, keepdims=True)
    total = None
    for block in range(blocks):
        at = slice(block * CHUNK, (block + 1) * CHUNK)
        shifted = jnp.exp2(twice * buffer[at] - top)
        buffer[at] = shifted
        part = jnp.sum(shifted.reshape(CHUNK // 8, 8, size), axis=0)
        total = part if total is None else total + part
    scale = 1.0 / jnp.sum(total, axis=0, keepdims=True)
    ones = jnp.ones((8, size), BF)
    for block in range(blocks):
        at = slice(block * CHUNK, (block + 1) * CHUNK)
        resp = (buffer[at] * scale).astype(BF)
        sums[at] = dot(resp, points, (1, 0))
        mass = dot(ones, resp, (1, 1))
        for k in range(CHUNK // lanes):
            totals[block * (CHUNK // lanes) + k] = mass[:, k * lanes : (k + 1) * lanes]

    core = where[1]
    for piece in range(keep.shape[0]):
        block = core * keep.shape[0] + piece
        keep[piece, :lanes, :] = sums[pl.ds(pl.multiple_of(block * lanes, lanes), lanes), :]
        keep[piece, lanes:, :] = jnp.broadcast_to(totals[block, 0:1], (16, lanes))
        block = (1 - core) * keep.shape[0] + piece
        out = sums[pl.ds(pl.multiple_of(block * lanes, lanes), lanes), :]
        send[piece, :lanes, :] = out.astype(BF)
        send[piece, lanes:, :] = pair(totals[block, 0:1]).astype(BF)


def pair(mass):
    high = mass.astype(BF).astype(F32)
    return jnp.concatenate([high, mass - high, jnp.zeros((14, mass.shape[1]), F32)], axis=0)


def cluster(where, product, upper, wide, pieces):
    rows, rank = product.shape
    count = wide.shape[0]
    parcel = (pieces, rank + 16, rank)
    vmem = pl.BlockSpec(memory_space=pltpu.VMEM)
    return pl.pallas_call(
        cluster_body,
        in_specs=[
            pl.BlockSpec(memory_space=pltpu.SMEM), vmem, vmem, pl.BlockSpec(memory_space=pl.ANY),
        ],
        out_shape=[
            jax.ShapeDtypeStruct((rows, rank), BF),
            pltpu.VMEM(parcel, F32),
            jax.ShapeDtypeStruct(parcel, BF),
        ],
        scratch_shapes=[
            pltpu.VMEM((count, rank), F32),
            pltpu.VMEM((count // rank, 8, rank), F32),
            pltpu.VMEM((count, rows), F32),
            pltpu.VMEM(wide.shape, BF),
            pltpu.SemaphoreType.DMA,
        ],
        name="cluster",
    )(where, near(product), near(upper), wide)


def pool_body(keep, got, out):
    lanes = out.shape[2]
    out[:, :lanes, :] = (keep[:, :lanes, :] + got[:, :lanes, :].astype(F32)).astype(BF)
    for piece in range(out.shape[0]):
        tail = got[piece, lanes:, :].astype(F32)
        mass = keep[piece, lanes : lanes + 1, :] + tail[0:1] + tail[1:2]
        out[piece, lanes:, :] = pair(mass).astype(BF)


def mass_body(parts, out):
    lanes = out.shape[1]
    total = jnp.sum(parts[...].astype(F32), axis=0)
    out[:lanes, :] = total[:lanes]
    out[lanes:, :] = jnp.broadcast_to(total[lanes : lanes + 1] + total[lanes + 1 : lanes + 2], (8, lanes))


def centers_body(where, first, second, third, fourth, centroids, out):
    stack = [part[...] for part in (first, second, third, fourth)]
    lanes = out.shape[2]
    total = jnp.zeros_like(stack[0])
    for y in range(SIDE):
        place = (where[0] + SIDE - y) % SIDE
        pick = stack[0]
        for k in range(1, SIDE):
            pick = jnp.where(place == k, stack[k], pick)
        total = total + pick
    column = jnp.transpose(jnp.broadcast_to(total[lanes : lanes + 1], (lanes, lanes)))
    values = ((total[:lanes] + centroids[...].astype(F32)) / (column + 1.0)).astype(BF)
    for copy in range(out.shape[0]):
        out[copy] = values


def join_body(where, mine, theirs, out):
    core = where[1]
    lanes = out.shape[2]
    for piece in range(mine.shape[0]):
        rows = slice(piece * lanes, (piece + 1) * lanes)
        out[core, rows, :] = mine[piece].astype(F32)
        out[1 - core, rows, :] = theirs[piece].astype(F32)


def shards(tiles, tile_list, tile_count, scale_index, scales, panel_start, centroids):
    block_size = tiles.shape[1]
    piece, rank = panel_start.shape
    rows_axis = lax.axis_size("row")
    cols_axis = lax.axis_size("col")
    total_rows = piece * rows_axis * cols_axis
    row_at = lax.axis_index("row")
    col_at = lax.axis_index("col")
    row_blocks = piece * cols_axis // block_size
    col_blocks = piece * rows_axis // block_size
    meta = jnp.concatenate(
        [
            tile_list[:, 0] - row_at * row_blocks,
            tile_list[:, 1] - col_at * col_blocks,
            tile_count,
            jnp.stack([col_at // 2, col_at % 2]).astype(jnp.int32),
        ]
    )
    where = jnp.stack([col_at // 2, col_at % 2, row_at]).astype(jnp.int32)
    table_ids = jnp.arange(scales.shape[0], dtype=jnp.int32)
    weights = jnp.sum(
        jnp.where(scale_index[:, None] == table_ids[None, :], scales[None, :], 0.0), axis=1
    )
    spot = pltpu.VMEM
    square = spot((rank, rank), F32)
    tall = spot((piece, rank), BF)
    tall_f32 = spot((piece, rank), F32)

    copies_shape = jax.ShapeDtypeStruct((rows_axis, rank, piece), BF)
    panel = panel_start
    gram = None
    for round_index in range(ROUNDS):
        last = round_index + 1 == ROUNDS
        shifted = [shift_col(panel, d, 0) for d in (1, 2, 3)]
        if gram is None:
            *shifted, meta, weights, where = lax.optimization_barrier(
                (*shifted, meta, weights, where)
            )
        else:
            gram = sum_x(gram)
            *shifted, gram = lax.optimization_barrier((*shifted, gram))
            gram = sum_z(gram)
        mine = jnp.stack([panel] + shifted)
        theirs = shift_col(mine, 0, 1)
        partial = tile_call(
            down_body, meta, weights, [mine, theirs], tiles, copies_shape,
            [pltpu.VMEM((col_blocks, rank, block_size), F32), pltpu.VMEM((block_size, rank), BF)],
        )
        if gram is None:
            parts = lax.all_to_all(partial, "row", 0, 0, tiled=True)
            copies, gram = small_call(reduce_first_body, [copies_shape, square], parts)
        else:
            partial, gram = lax.optimization_barrier((partial, gram))
            parts = lax.all_to_all(partial, "row", 0, 0, tiled=True)
            gram = sum_y(gram)
            upper = factor_of(total_rows, gram, shift_col(gram, 0, 1))
            copies, gram = small_call(reduce_down_body, [copies_shape, square], parts, upper, far=1)
        gathered = lax.all_to_all(copies, "row", 0, 0, tiled=True)
        gram = sum_y(gram)
        gram = sum_x(gram + shift_col(gram, 0, 1))
        if last:
            source, _ = lax.optimization_barrier((centroids, copies))
            wide = small_call(
                widen_body, jax.ShapeDtypeStruct((centroids.shape[0], 2 * rank), BF),
                source, far=1,
            )
            owner = (where[1] * rows_axis + where[2]) * rank
            owned = lax.dynamic_slice_in_dim(source, owner, rank, 0)
            gathered, wide, owned = lax.optimization_barrier((gathered, wide, owned))
        gathered, gram = lax.optimization_barrier((gathered, gram))
        grams = ring(gram, lambda v, d: shift_row(v, 0, d))
        keep, send = tile_call(
            up_body, meta, weights, [gathered], tiles,
            [jax.ShapeDtypeStruct((SIDE, piece, rank), F32)] * 2,
            [pltpu.VMEM((row_blocks, block_size, rank), F32)],
        )
        got = shift_col(send, 0, 1)
        own, one, two, three = small_call(
            fold_body, [tall_f32, tall, tall, tall], keep, got, where=where,
            far=1,
        )
        *grams, own = lax.optimization_barrier((*grams, own))
        upper = factor_of(total_rows, *grams)
        one, two, three = shift_col(one, 1, 0), shift_col(two, 2, 0), shift_col(three, 3, 0)
        panel, gram = small_call(
            reduce_last_body if last else reduce_up_body,
            [tall_f32 if last else tall, square], own, one, two, three, upper,
        )
    gram = sum_y(gram + shift_col(gram, 0, 1))
    upper = factor_of(total_rows, *ring(sum_x(gram), lambda v, d: shift_row(v, 0, d)))

    panel, keep, send = cluster(where, panel, upper, wide, rows_axis)
    got = shift_col(send, 0, 1)
    packed = small_call(pool_body, spot(send.shape, BF), keep, got)
    parts = lax.all_to_all(packed, "row", 0, 0, tiled=True)
    mass = small_call(mass_body, spot((rank + 8, rank), F32), parts)
    masses = [mass] + [shift_col(mass, d, 0) for d in (1, 2, 3)]
    copies = small_call(
        centers_body, jax.ShapeDtypeStruct((rows_axis, rank, rank), BF), *masses, owned,
        where=where,
    )
    mine = lax.all_to_all(copies, "row", 0, 0, tiled=True)
    theirs = shift_col(mine, 0, 1)
    count = centroids.shape[0]
    centers = small_call(
        join_body, jax.ShapeDtypeStruct((2, count // 2, rank), F32), mine, theirs,
        where=where,
    )
    return (panel, centers.reshape(count, rank))


def solution(mesh):
    return jax.shard_map(
        shards,
        mesh=mesh,
        in_specs=(
            P(("row", "col"), None, None),
            P(("row", "col"), None),
            P(("row", "col")),
            P(("row", "col")),
            P(),
            P(("row", "col"), None),
            P(),
        ),
        out_specs=(P(("row", "col"), None), P()),
        check_vma=False,
    )
```

```python
import functools
import math

import jax
import jax.numpy as jnp
from jax import lax
from jax.experimental import pallas as pl
from jax.experimental.pallas import tpu as pltpu
from jax.sharding import PartitionSpec as P

ROUNDS = 2
SHARPNESS = 48.0
EPS = 1e-06
CLOSE = 1e-05
CHUNK = 512

SIDE = 4
BF = jnp.bfloat16
F32 = jnp.float32
HIGHEST = lax.Precision.HIGHEST


def dot(a, b, contract, precision=None):
    return lax.dot_general(
        a, b, ((contract[:1], contract[1:]), ((), ())), precision=precision,
        preferred_element_type=F32,
    )


def shift_row(value, dx, dz):
    pairs = [
        (x * SIDE + z, (x + dx) % SIDE * SIDE + (z + dz) % SIDE)
        for x in range(SIDE)
        for z in range(SIDE)
    ]
    return lax.ppermute(value, "row", pairs)


def shift_col(value, dy, dc):
    pairs = [
        (y * 2 + c, (y + dy) % SIDE * 2 + (c + dc) % 2) for y in range(SIDE) for c in range(2)
    ]
    return lax.ppermute(value, "col", pairs)


def near(value):
    return pltpu.with_memory_space_constraint(value, pltpu.VMEM)


def small_call(body, out_shapes, *args, where=None, scratch=(), far=0):
    scalars = [] if where is None else [where]
    return pl.pallas_call(
        body,
        in_specs=[pl.BlockSpec(memory_space=pltpu.SMEM)] * len(scalars)
        + [pl.BlockSpec(memory_space=pltpu.VMEM)] * len(args),
        out_shape=out_shapes,
        scratch_shapes=scratch,
    )(*scalars, *args[:far], *(near(arg) for arg in args[far:]))


def each_tile(meta, tiles, buffers, arrivals, acc, add):
    def load(slot):
        return pltpu.make_async_copy(tiles.at[slot], buffers.at[slot], arrivals.at[slot])

    def start(slot, carry):
        load(slot).start()
        return carry

    def finish(slot, carry):
        load(slot).wait()
        add(slot)
        return carry

    lax.fori_loop(0, meta[12], start, 0)
    acc[...] = jnp.zeros_like(acc)
    lax.fori_loop(0, meta[12], finish, 0)


def down_body(meta, weights, mine, theirs, tiles, out, acc, rows, stage, buffers, arrivals, leave):
    half = mine.shape[1]
    core = meta[14]

    def add(slot):
        place = (meta[13] + SIDE - meta[slot]) % SIDE
        rows[pl.ds(pl.multiple_of(core * half, half), half), :] = mine[place]
        rows[pl.ds(pl.multiple_of((1 - core) * half, half), half), :] = theirs[place]
        product = dot(rows[...], buffers[slot], (0, 0))
        target = meta[6 + slot]
        acc[target] = acc[target] + weights[slot] * product

    each_tile(meta, tiles, buffers, arrivals, acc, add)
    sends = []
    for block in range(acc.shape[0]):
        pair_of = pl.ds(2 * block, 2)
        stage[2 * block] = acc[block, :, :half].astype(BF)
        stage[2 * block + 1] = acc[block, :, half:].astype(BF)
        sends.append(pltpu.make_async_copy(stage.at[pair_of], out.at[pair_of], leave.at[block]))
        sends[-1].start()
    for send in sends:
        send.wait()


def up_body(meta, weights, gathered, tiles, keep, send, acc, buffers, arrivals, leave):
    half = gathered.shape[2]
    core = meta[14]

    def add(slot):
        source = meta[6 + slot]
        product = dot(buffers[slot, :, :half], gathered[2 * source], (1, 1))
        product += dot(buffers[slot, :, half:], gathered[2 * source + 1], (1, 1))
        target = meta[slot]
        acc[target] = acc[target] + weights[slot] * product

    each_tile(meta, tiles, buffers, arrivals, acc, add)
    sends = []
    for side, target in enumerate((send, keep)):
        at = pl.ds(pl.multiple_of((core if side else 1 - core) * half, half), half)
        sends.append(pltpu.make_async_copy(acc.at[:, at, :], target, leave.at[side]))
        sends[-1].start()
    for move in sends:
        move.wait()


def tile_call(body, meta, weights, panels, tiles, outs, scratch):
    slots, block, _ = tiles.shape
    return pl.pallas_call(
        body,
        in_specs=[pl.BlockSpec(memory_space=pltpu.SMEM)] * 2
        + [pl.BlockSpec(memory_space=pltpu.VMEM)] * len(panels)
        + [pl.BlockSpec(memory_space=pl.ANY)],
        out_specs=jax.tree.map(lambda out: pl.BlockSpec(memory_space=pl.ANY), outs),
        out_shape=outs,
        scratch_shapes=scratch
        + [
            pltpu.VMEM(tiles.shape, BF),
            pltpu.SemaphoreType.DMA((slots,)),
            pltpu.SemaphoreType.DMA((8,)),
        ],
        cost_estimate=pl.CostEstimate(
            flops=2 * slots * block * block * 128,
            transcendentals=0,
            bytes_accessed=slots * block * block * 2 + 4 * 1024 * 1024,
        ),
    )(meta, weights, *(near(panel) for panel in panels), tiles)


def share_wide(total, out, gram):
    factor = total.astype(BF)
    for copy in range(out.shape[0]):
        out[copy] = factor
    gram[...] = packed(dot(factor, factor, (1, 1)))


def reduce_first_body(parts, out, gram):
    share_wide(jnp.sum(parts[...].astype(F32), axis=0), out, gram)


def reduce_down_body(parts, upper, out, gram):
    total = jnp.sum(parts[...].astype(F32), axis=0)
    share_wide(dot(upper[...], total, (0, 0), HIGHEST), out, gram)


def fold_body(where, keep, got, own, one, two, three):
    at = where[0]
    own[...] = keep[at] + got[at]
    for distance, out in ((1, one), (2, two), (3, three)):
        to = (at + distance) % SIDE
        out[...] = (keep[to] + got[to]).astype(BF)


def reduce_up_body(own, one, two, three, upper, out, gram):
    total = own[...] + one[...].astype(F32) + two[...].astype(F32) + three[...].astype(F32)
    panel = dot(total, upper[...], (1, 0), HIGHEST).astype(BF)
    out[...] = panel
    gram[...] = packed(dot(panel, panel, (0, 0)))


def reduce_last_body(own, one, two, three, upper, out, gram):
    total = own[...] + one[...].astype(F32) + two[...].astype(F32) + three[...].astype(F32)
    total = dot(total, upper[...], (1, 0), HIGHEST)
    out[...] = total
    gram[...] = packed(dot(total, total, (0, 0), HIGHEST))


def packed(gram):
    half = gram.shape[0] // 2
    last = gram[half:, half:]
    beside = jnp.concatenate([last[: half // 2], last[half // 2 :]], axis=1)
    return jnp.concatenate([gram[:half], beside], axis=0)


def unpacked(value):
    half = value.shape[1] // 2
    last = jnp.concatenate([value[half:, :half], value[half:, half:]], axis=0)
    low = jnp.concatenate([jnp.transpose(value[:half, half:]), last], axis=1)
    return jnp.concatenate([value[:half], low], axis=0)


def factor_body(total_rows, *refs):
    *grams, out, work, build = refs
    gram = unpacked(sum(part[...] for part in grams)) / total_rows
    size = gram.shape[0]
    down = lax.broadcasted_iota(jnp.int32, (size, size), 0)
    across = lax.broadcasted_iota(jnp.int32, (size, size), 1)
    eye = jnp.where(down == across, 1.0, 0.0).astype(F32)
    keep = jnp.where(down < across, 1.0, 0.5 * eye)
    diagonal = gram * eye
    tall = lax.rsqrt(jnp.sum(diagonal, axis=1, keepdims=True))
    scaled = gram * tall * lax.rsqrt(jnp.sum(diagonal, axis=0, keepdims=True))
    build[...] = eye - keep * (scaled - eye)

    def refine(state):
        at, _ = state
        guess = build[...]
        excess = dot(guess, dot(scaled, guess, (1, 0), HIGHEST), (0, 0), HIGHEST) - eye
        build[...] = guess - dot(guess, keep * excess, (1, 0), HIGHEST)
        return at + 1, jnp.max(jnp.abs(excess))

    def unfinished(state):
        at, error = state
        return (at < 10) & jnp.logical_not(error < CLOSE)

    _, error = lax.while_loop(unfinished, refine, (jnp.int32(0), jnp.float32(1.0)))
    out[...] = build[...] * tall

    @pl.when(jnp.logical_not(error < CLOSE))
    def _():
        work[...] = gram
        build[...] = eye

        def eliminate(k, carry):
            row = work[pl.ds(k, 1), :]
            pivot = jnp.sum(jnp.where(across[:1] == k, row, 0.0), axis=1, keepdims=True)
            column = jnp.sum(jnp.where(across == k, work[...], 0.0), axis=1, keepdims=True)
            ratio = jnp.where(down[:, :1] > k, column / pivot, 0.0)
            unit = build[pl.ds(k, 1), :]
            work[...] = work[...] - ratio * row
            build[...] = build[...] - ratio * unit
            return carry

        lax.fori_loop(0, size, eliminate, 0)
        pivots = jnp.sum(work[...] * eye, axis=1, keepdims=True)
        out[...] = jnp.transpose(build[...] * lax.rsqrt(pivots))


def ring(value, shift):
    return [value] + [shift(value, d) for d in (1, 2, 3)]


def ring_sum(value, shift):
    return sum(ring(value, shift))


def sum_x(value):
    return ring_sum(value, lambda v, d: shift_row(v, d, 0))


def sum_z(value):
    return ring_sum(value, lambda v, d: shift_row(v, 0, d))


def sum_y(value):
    return ring_sum(value, lambda v, d: shift_col(v, d, 0))


def factor_of(total_rows, *grams):
    gram = grams[0]
    return small_call(
        functools.partial(factor_body, total_rows),
        pltpu.VMEM((gram.shape[1],) * 2, F32), *grams,
        scratch=[pltpu.VMEM((gram.shape[1],) * 2, F32)] * 2,
    )


def widen_body(centroids, out):
    count, lanes = centroids.shape
    values = centroids[...].astype(F32)
    norms = -0.5 * jnp.sum(values * values, axis=1, keepdims=True)
    high = norms.astype(BF).astype(F32)
    middle = (norms - high).astype(BF).astype(F32)
    lane = lax.broadcasted_iota(jnp.int32, (count, lanes), 1)
    parts = jnp.where(lane == 2, norms - high - middle, 0.0)
    parts = jnp.where(lane == 1, middle, parts)
    out[:, :lanes] = centroids[...]
    out[:, lanes:] = jnp.where(lane == 0, high, parts).astype(BF)


def cluster_body(where, product, upper, source, panel, keep, send, sums, totals, buffer, wide, arrival):
    load = pltpu.make_async_copy(source, wide, arrival)
    load.start()
    twice = 2.0 * SHARPNESS * math.log2(math.e)
    count, lanes = sums.shape
    blocks = count // CHUNK
    rows = dot(product[...], upper[...], (1, 0), HIGHEST).astype(BF)
    panel[...] = rows
    values = rows.astype(F32)
    length = jnp.sqrt(jnp.sum(values * values, axis=1, keepdims=True) + EPS)
    points = (values / length).astype(BF)
    size = points.shape[0]
    lane = lax.broadcasted_iota(jnp.int32, points.shape, 1)
    wide_points = jnp.concatenate([points, jnp.where(lane < 3, 1.0, 0.0).astype(BF)], axis=1)
    load.wait()

    top = None
    for block in range(blocks):
        at = slice(block * CHUNK, (block + 1) * CHUNK)
        scores = dot(wide[at], wide_points, (1, 1))
        buffer[at] = scores
        most = jnp.max(scores.reshape(CHUNK // 8, 8, size), axis=0)
        top = most if top is None else jnp.maximum(top, most)
    top = twice * jnp.max(top, axis=0, keepdims=True)
    total = None
    for block in range(blocks):
        at = slice(block * CHUNK, (block + 1) * CHUNK)
        shifted = jnp.exp2(twice * buffer[at] - top)
        buffer[at] = shifted
        part = jnp.sum(shifted.reshape(CHUNK // 8, 8, size), axis=0)
        total = part if total is None else total + part
    scale = 1.0 / jnp.sum(total, axis=0, keepdims=True)
    ones = jnp.ones((8, size), BF)
    for block in range(blocks):
        at = slice(block * CHUNK, (block + 1) * CHUNK)
        resp = (buffer[at] * scale).astype(BF)
        sums[at] = dot(resp, points, (1, 0))
        mass = dot(ones, resp, (1, 1))
        for k in range(CHUNK // lanes):
            totals[block * (CHUNK // lanes) + k] = mass[:, k * lanes : (k + 1) * lanes]

    core = where[1]
    for piece in range(keep.shape[0]):
        block = core * keep.shape[0] + piece
        keep[piece, :lanes, :] = sums[pl.ds(pl.multiple_of(block * lanes, lanes), lanes), :]
        keep[piece, lanes:, :] = jnp.broadcast_to(totals[block, 0:1], (16, lanes))
        block = (1 - core) * keep.shape[0] + piece
        out = sums[pl.ds(pl.multiple_of(block * lanes, lanes), lanes), :]
        send[piece, :lanes, :] = out.astype(BF)
        send[piece, lanes:, :] = pair(totals[block, 0:1]).astype(BF)


def pair(mass):
    high = mass.astype(BF).astype(F32)
    return jnp.concatenate([high, mass - high, jnp.zeros((14, mass.shape[1]), F32)], axis=0)


def cluster(where, product, upper, wide, pieces):
    rows, rank = product.shape
    count = wide.shape[0]
    parcel = (pieces, rank + 16, rank)
    vmem = pl.BlockSpec(memory_space=pltpu.VMEM)
    return pl.pallas_call(
        cluster_body,
        in_specs=[
            pl.BlockSpec(memory_space=pltpu.SMEM), vmem, vmem, pl.BlockSpec(memory_space=pl.ANY),
        ],
        out_shape=[
            jax.ShapeDtypeStruct((rows, rank), BF),
            pltpu.VMEM(parcel, F32),
            jax.ShapeDtypeStruct(parcel, BF),
        ],
        scratch_shapes=[
            pltpu.VMEM((count, rank), F32),
            pltpu.VMEM((count // rank, 8, rank), F32),
            pltpu.VMEM((count, rows), F32),
            pltpu.VMEM(wide.shape, BF),
            pltpu.SemaphoreType.DMA,
        ],
        name="cluster",
    )(where, near(product), near(upper), wide)


def pool_body(keep, got, out):
    lanes = out.shape[2]
    out[:, :lanes, :] = (keep[:, :lanes, :] + got[:, :lanes, :].astype(F32)).astype(BF)
    for piece in range(out.shape[0]):
        tail = got[piece, lanes:, :].astype(F32)
        mass = keep[piece, lanes : lanes + 1, :] + tail[0:1] + tail[1:2]
        out[piece, lanes:, :] = pair(mass).astype(BF)


def mass_body(parts, out):
    lanes = out.shape[1]
    total = jnp.sum(parts[...].astype(F32), axis=0)
    out[:lanes, :] = total[:lanes]
    out[lanes:, :] = jnp.broadcast_to(total[lanes : lanes + 1] + total[lanes + 1 : lanes + 2], (8, lanes))


def centers_body(where, first, second, third, fourth, centroids, out):
    stack = [part[...] for part in (first, second, third, fourth)]
    lanes = out.shape[2]
    total = jnp.zeros_like(stack[0])
    for y in range(SIDE):
        place = (where[0] + SIDE - y) % SIDE
        pick = stack[0]
        for k in range(1, SIDE):
            pick = jnp.where(place == k, stack[k], pick)
        total = total + pick
    column = jnp.transpose(jnp.broadcast_to(total[lanes : lanes + 1], (lanes, lanes)))
    values = ((total[:lanes] + centroids[...].astype(F32)) / (column + 1.0)).astype(BF)
    for copy in range(out.shape[0]):
        out[copy] = values


def join_body(where, mine, theirs, out):
    core = where[1]
    lanes = out.shape[2]
    for piece in range(mine.shape[0]):
        rows = slice(piece * lanes, (piece + 1) * lanes)
        out[core, rows, :] = mine[piece].astype(F32)
        out[1 - core, rows, :] = theirs[piece].astype(F32)


def shards(tiles, tile_list, tile_count, scale_index, scales, panel_start, centroids):
    block_size = tiles.shape[1]
    piece, rank = panel_start.shape
    rows_axis = lax.axis_size("row")
    cols_axis = lax.axis_size("col")
    total_rows = piece * rows_axis * cols_axis
    row_at = lax.axis_index("row")
    col_at = lax.axis_index("col")
    row_blocks = piece * cols_axis // block_size
    col_blocks = piece * rows_axis // block_size
    meta = jnp.concatenate(
        [
            tile_list[:, 0] - row_at * row_blocks,
            tile_list[:, 1] - col_at * col_blocks,
            tile_count,
            jnp.stack([col_at // 2, col_at % 2]).astype(jnp.int32),
        ]
    )
    where = jnp.stack([col_at // 2, col_at % 2, row_at]).astype(jnp.int32)
    table_ids = jnp.arange(scales.shape[0], dtype=jnp.int32)
    weights = jnp.sum(
        jnp.where(scale_index[:, None] == table_ids[None, :], scales[None, :], 0.0), axis=1
    )
    spot = pltpu.VMEM
    square = spot((rank * 3 // 4, rank), F32)
    tall = spot((piece, rank), BF)
    tall_f32 = spot((piece, rank), F32)

    copies_shape = jax.ShapeDtypeStruct((rows_axis, rank, piece), BF)
    panel = panel_start
    gram = None
    for round_index in range(ROUNDS):
        last = round_index + 1 == ROUNDS
        shifted = [shift_col(panel, d, 0) for d in (1, 2, 3)]
        if gram is None:
            *shifted, meta, weights, where = lax.optimization_barrier(
                (*shifted, meta, weights, where)
            )
        else:
            gram = sum_x(gram)
            *shifted, gram = lax.optimization_barrier((*shifted, gram))
            gram = sum_z(gram)
        mine = jnp.stack([panel] + shifted)
        theirs = shift_col(mine, 0, 1)
        partial = tile_call(
            down_body, meta, weights, [mine, theirs], tiles, copies_shape,
            [
                pltpu.VMEM((col_blocks, rank, block_size), F32),
                pltpu.VMEM((block_size, rank), BF),
                pltpu.VMEM((rows_axis, rank, piece), BF),
            ],
        )
        if gram is None:
            parts = lax.all_to_all(partial, "row", 0, 0, tiled=True)
            copies, gram = small_call(reduce_first_body, [copies_shape, square], parts)
        else:
            partial, gram = lax.optimization_barrier((partial, gram))
            parts = lax.all_to_all(partial, "row", 0, 0, tiled=True)
            gram = sum_y(gram)
            upper = factor_of(total_rows, gram, shift_col(gram, 0, 1))
            copies, gram = small_call(reduce_down_body, [copies_shape, square], parts, upper, far=1)
        gathered = lax.all_to_all(copies, "row", 0, 0, tiled=True)
        gram = sum_y(gram)
        gram = sum_x(gram + shift_col(gram, 0, 1))
        if last:
            source, _ = lax.optimization_barrier((centroids, copies))
            wide = small_call(
                widen_body, jax.ShapeDtypeStruct((centroids.shape[0], 2 * rank), BF),
                source, far=1,
            )
            owner = (where[1] * rows_axis + where[2]) * rank
            owned = lax.dynamic_slice_in_dim(source, owner, rank, 0)
            gathered, wide, owned = lax.optimization_barrier((gathered, wide, owned))
        gathered, gram = lax.optimization_barrier((gathered, gram))
        grams = ring(gram, lambda v, d: shift_row(v, 0, d))
        keep, send = tile_call(
            up_body, meta, weights, [gathered], tiles,
            [jax.ShapeDtypeStruct((SIDE, piece, rank), F32)] * 2,
            [pltpu.VMEM((row_blocks, block_size, rank), F32)],
        )
        *grams, got = lax.optimization_barrier((*grams, shift_col(send, 0, 1)))
        own, one, two, three = small_call(
            fold_body, [tall_f32, tall, tall, tall], keep, got, where=where,
            far=1,
        )
        *grams, own = lax.optimization_barrier((*grams, own))
        upper = factor_of(total_rows, *grams)
        one, two, three = shift_col(one, 1, 0), shift_col(two, 2, 0), shift_col(three, 3, 0)
        panel, gram = small_call(
            reduce_last_body if last else reduce_up_body,
            [tall_f32 if last else tall, square], own, one, two, three, upper,
        )
    gram = sum_y(gram + shift_col(gram, 0, 1))
    upper = factor_of(total_rows, *ring(sum_x(gram), lambda v, d: shift_row(v, 0, d)))

    panel, keep, send = cluster(where, panel, upper, wide, rows_axis)
    got = shift_col(send, 0, 1)
    packed = small_call(pool_body, spot(send.shape, BF), keep, got)
    parts = lax.all_to_all(packed, "row", 0, 0, tiled=True)
    mass = small_call(mass_body, spot((rank + 8, rank), F32), parts)
    masses = [mass] + [shift_col(mass, d, 0) for d in (1, 2, 3)]
    copies = small_call(
        centers_body, jax.ShapeDtypeStruct((rows_axis, rank, rank), BF), *masses, owned,
        where=where,
    )
    mine = lax.all_to_all(copies, "row", 0, 0, tiled=True)
    theirs = shift_col(mine, 0, 1)
    count = centroids.shape[0]
    centers = small_call(
        join_body, jax.ShapeDtypeStruct((2, count // 2, rank), F32), mine, theirs,
        where=where,
    )
    return (panel, centers.reshape(count, rank))


def solution(mesh):
    return jax.shard_map(
        shards,
        mesh=mesh,
        in_specs=(
            P(("row", "col"), None, None),
            P(("row", "col"), None),
            P(("row", "col")),
            P(("row", "col")),
            P(),
            P(("row", "col"), None),
            P(),
        ),
        out_specs=(P(("row", "col"), None), P()),
        check_vma=False,
    )
```

```python
import functools
import math

import jax
import jax.numpy as jnp
from jax import lax
from jax.experimental import pallas as pl
from jax.experimental.pallas import tpu as pltpu
from jax.sharding import PartitionSpec as P

ROUNDS = 2
SHARPNESS = 48.0
EPS = 1e-06
CLOSE = 1e-05
CHUNK = 512

SIDE = 4
BF = jnp.bfloat16
F32 = jnp.float32
HIGHEST = lax.Precision.HIGHEST


def dot(a, b, contract, precision=None):
    return lax.dot_general(
        a, b, ((contract[:1], contract[1:]), ((), ())), precision=precision,
        preferred_element_type=F32,
    )


def shift_row(value, dx, dz):
    pairs = [
        (x * SIDE + z, (x + dx) % SIDE * SIDE + (z + dz) % SIDE)
        for x in range(SIDE)
        for z in range(SIDE)
    ]
    return lax.ppermute(value, "row", pairs)


def shift_col(value, dy, dc):
    pairs = [
        (y * 2 + c, (y + dy) % SIDE * 2 + (c + dc) % 2) for y in range(SIDE) for c in range(2)
    ]
    return lax.ppermute(value, "col", pairs)


def near(value):
    return pltpu.with_memory_space_constraint(value, pltpu.VMEM)


def small_call(body, out_shapes, *args, where=None, scratch=(), far=0):
    scalars = [] if where is None else [where]
    return pl.pallas_call(
        body,
        in_specs=[pl.BlockSpec(memory_space=pltpu.SMEM)] * len(scalars)
        + [pl.BlockSpec(memory_space=pltpu.VMEM)] * len(args),
        out_shape=out_shapes,
        scratch_shapes=scratch,
    )(*scalars, *args[:far], *(near(arg) for arg in args[far:]))


def each_tile(meta, tiles, buffers, arrivals, acc, add):
    def load(slot):
        return pltpu.make_async_copy(tiles.at[slot], buffers.at[slot], arrivals.at[slot])

    def start(slot, carry):
        load(slot).start()
        return carry

    def finish(slot, carry):
        load(slot).wait()
        add(slot)
        return carry

    lax.fori_loop(0, meta[12], start, 0)
    acc[...] = jnp.zeros_like(acc)
    lax.fori_loop(0, meta[12], finish, 0)


def down_body(meta, weights, mine, theirs, tiles, out, acc, rows, stage, buffers, arrivals, leave):
    half = mine.shape[1]
    core = meta[14]

    def add(slot):
        place = (meta[13] + SIDE - meta[slot]) % SIDE
        rows[pl.ds(pl.multiple_of(core * half, half), half), :] = mine[place]
        rows[pl.ds(pl.multiple_of((1 - core) * half, half), half), :] = theirs[place]
        product = dot(rows[...], buffers[slot], (0, 0))
        target = meta[6 + slot]
        acc[target] = acc[target] + weights[slot] * product

    each_tile(meta, tiles, buffers, arrivals, acc, add)
    sends = []
    for block in range(acc.shape[0]):
        pair_of = pl.ds(2 * block, 2)
        stage[2 * block] = acc[block, :, :half].astype(BF)
        stage[2 * block + 1] = acc[block, :, half:].astype(BF)
        sends.append(pltpu.make_async_copy(stage.at[pair_of], out.at[pair_of], leave.at[block]))
        sends[-1].start()
    for send in sends:
        send.wait()


def up_body(meta, weights, gathered, tiles, keep, send, acc, buffers, arrivals, leave):
    half = gathered.shape[2]
    core = meta[14]

    def add(slot):
        source = meta[6 + slot]
        product = dot(buffers[slot, :, :half], gathered[2 * source], (1, 1))
        product += dot(buffers[slot, :, half:], gathered[2 * source + 1], (1, 1))
        target = meta[slot]
        acc[target] = acc[target] + weights[slot] * product

    each_tile(meta, tiles, buffers, arrivals, acc, add)
    sends = []
    for side, target in enumerate((send, keep)):
        at = pl.ds(pl.multiple_of((core if side else 1 - core) * half, half), half)
        sends.append(pltpu.make_async_copy(acc.at[:, at, :], target, leave.at[side]))
        sends[-1].start()
    for move in sends:
        move.wait()


def tile_call(body, meta, weights, panels, tiles, outs, scratch):
    slots, block, _ = tiles.shape
    return pl.pallas_call(
        body,
        in_specs=[pl.BlockSpec(memory_space=pltpu.SMEM)] * 2
        + [pl.BlockSpec(memory_space=pltpu.VMEM)] * len(panels)
        + [pl.BlockSpec(memory_space=pl.ANY)],
        out_specs=jax.tree.map(lambda out: pl.BlockSpec(memory_space=pl.ANY), outs),
        out_shape=outs,
        scratch_shapes=scratch
        + [
            pltpu.VMEM(tiles.shape, BF),
            pltpu.SemaphoreType.DMA((slots,)),
            pltpu.SemaphoreType.DMA((8,)),
        ],
        cost_estimate=pl.CostEstimate(
            flops=2 * slots * block * block * 128,
            transcendentals=0,
            bytes_accessed=slots * block * block * 2 + 4 * 1024 * 1024,
        ),
    )(meta, weights, *(near(panel) for panel in panels), tiles)


def share_wide(total, out, gram):
    factor = total.astype(BF)
    for copy in range(out.shape[0]):
        out[copy] = factor
    gram[...] = packed(dot(factor, factor, (1, 1)))


def reduce_first_body(parts, out, gram):
    share_wide(jnp.sum(parts[...].astype(F32), axis=0), out, gram)


def reduce_down_body(parts, upper, out, gram, stage, arrivals):
    loads = [
        pltpu.make_async_copy(parts.at[part], stage.at[part], arrivals.at[part])
        for part in range(parts.shape[0])
    ]
    for load in loads:
        load.start()
    total = None
    for part, load in enumerate(loads):
        load.wait()
        value = stage[part].astype(F32)
        total = value if total is None else total + value
    share_wide(dot(upper[...], total, (0, 0), HIGHEST), out, gram)


def fold_body(where, keep, got, own, one, two, three):
    at = where[0]
    own[...] = keep[at] + got[at]
    for distance, out in ((1, one), (2, two), (3, three)):
        to = (at + distance) % SIDE
        out[...] = (keep[to] + got[to]).astype(BF)


def reduce_up_body(own, one, two, three, upper, out, gram):
    total = own[...] + one[...].astype(F32) + two[...].astype(F32) + three[...].astype(F32)
    panel = dot(total, upper[...], (1, 0), HIGHEST).astype(BF)
    out[...] = panel
    gram[...] = packed(dot(panel, panel, (0, 0)))


def reduce_last_body(own, one, two, three, upper, out, gram):
    total = own[...] + one[...].astype(F32) + two[...].astype(F32) + three[...].astype(F32)
    total = dot(total, upper[...], (1, 0), HIGHEST)
    out[...] = total
    gram[...] = packed(dot(total, total, (0, 0), HIGHEST))


def packed(gram):
    half = gram.shape[0] // 2
    last = gram[half:, half:]
    beside = jnp.concatenate([last[: half // 2], last[half // 2 :]], axis=1)
    return jnp.concatenate([gram[:half], beside], axis=0)


def unpacked(value):
    half = value.shape[1] // 2
    last = jnp.concatenate([value[half:, :half], value[half:, half:]], axis=0)
    low = jnp.concatenate([jnp.transpose(value[:half, half:]), last], axis=1)
    return jnp.concatenate([value[:half], low], axis=0)


def factor_body(total_rows, *refs):
    *grams, out, work, build = refs
    gram = unpacked(sum(part[...] for part in grams)) / total_rows
    size = gram.shape[0]
    down = lax.broadcasted_iota(jnp.int32, (size, size), 0)
    across = lax.broadcasted_iota(jnp.int32, (size, size), 1)
    eye = jnp.where(down == across, 1.0, 0.0).astype(F32)
    keep = jnp.where(down < across, 1.0, 0.5 * eye)
    diagonal = gram * eye
    tall = lax.rsqrt(jnp.sum(diagonal, axis=1, keepdims=True))
    scaled = gram * tall * lax.rsqrt(jnp.sum(diagonal, axis=0, keepdims=True))
    build[...] = eye - keep * (scaled - eye)

    def refine(state):
        at, _ = state
        guess = build[...]
        excess = dot(guess, dot(scaled, guess, (1, 0), HIGHEST), (0, 0), HIGHEST) - eye
        build[...] = guess - dot(guess, keep * excess, (1, 0), HIGHEST)
        return at + 1, jnp.max(jnp.abs(excess))

    def unfinished(state):
        at, error = state
        return (at < 10) & jnp.logical_not(error < CLOSE)

    _, error = lax.while_loop(unfinished, refine, (jnp.int32(0), jnp.float32(1.0)))
    out[...] = build[...] * tall

    @pl.when(jnp.logical_not(error < CLOSE))
    def _():
        work[...] = gram
        build[...] = eye

        def eliminate(k, carry):
            row = work[pl.ds(k, 1), :]
            pivot = jnp.sum(jnp.where(across[:1] == k, row, 0.0), axis=1, keepdims=True)
            column = jnp.sum(jnp.where(across == k, work[...], 0.0), axis=1, keepdims=True)
            ratio = jnp.where(down[:, :1] > k, column / pivot, 0.0)
            unit = build[pl.ds(k, 1), :]
            work[...] = work[...] - ratio * row
            build[...] = build[...] - ratio * unit
            return carry

        lax.fori_loop(0, size, eliminate, 0)
        pivots = jnp.sum(work[...] * eye, axis=1, keepdims=True)
        out[...] = jnp.transpose(build[...] * lax.rsqrt(pivots))


def ring(value, shift):
    return [value] + [shift(value, d) for d in (1, 2, 3)]


def ring_sum(value, shift):
    return sum(ring(value, shift))


def sum_x(value):
    return ring_sum(value, lambda v, d: shift_row(v, d, 0))


def sum_z(value):
    return ring_sum(value, lambda v, d: shift_row(v, 0, d))


def sum_y(value):
    return ring_sum(value, lambda v, d: shift_col(v, d, 0))


def factor_of(total_rows, *grams):
    gram = grams[0]
    return small_call(
        functools.partial(factor_body, total_rows),
        pltpu.VMEM((gram.shape[1],) * 2, F32), *grams,
        scratch=[pltpu.VMEM((gram.shape[1],) * 2, F32)] * 2,
    )


def widen_body(centroids, out):
    count, lanes = centroids.shape
    values = centroids[...].astype(F32)
    norms = -0.5 * jnp.sum(values * values, axis=1, keepdims=True)
    high = norms.astype(BF).astype(F32)
    middle = (norms - high).astype(BF).astype(F32)
    lane = lax.broadcasted_iota(jnp.int32, (count, lanes), 1)
    parts = jnp.where(lane == 2, norms - high - middle, 0.0)
    parts = jnp.where(lane == 1, middle, parts)
    out[:, :lanes] = centroids[...]
    out[:, lanes:] = jnp.where(lane == 0, high, parts).astype(BF)


def cluster_body(where, product, upper, source, panel, keep, send, sums, totals, buffer, wide, arrival):
    load = pltpu.make_async_copy(source, wide, arrival)
    load.start()
    twice = 2.0 * SHARPNESS * math.log2(math.e)
    count, lanes = sums.shape
    blocks = count // CHUNK
    rows = dot(product[...], upper[...], (1, 0), HIGHEST).astype(BF)
    panel[...] = rows
    values = rows.astype(F32)
    length = jnp.sqrt(jnp.sum(values * values, axis=1, keepdims=True) + EPS)
    points = (values / length).astype(BF)
    size = points.shape[0]
    lane = lax.broadcasted_iota(jnp.int32, points.shape, 1)
    wide_points = jnp.concatenate([points, jnp.where(lane < 3, 1.0, 0.0).astype(BF)], axis=1)
    load.wait()

    top = None
    for block in range(blocks):
        at = slice(block * CHUNK, (block + 1) * CHUNK)
        scores = dot(wide[at], wide_points, (1, 1))
        buffer[at] = scores
        most = jnp.max(scores.reshape(CHUNK // 8, 8, size), axis=0)
        top = most if top is None else jnp.maximum(top, most)
    top = twice * jnp.max(top, axis=0, keepdims=True)
    total = None
    for block in range(blocks):
        at = slice(block * CHUNK, (block + 1) * CHUNK)
        shifted = jnp.exp2(twice * buffer[at] - top)
        buffer[at] = shifted
        part = jnp.sum(shifted.reshape(CHUNK // 8, 8, size), axis=0)
        total = part if total is None else total + part
    scale = 1.0 / jnp.sum(total, axis=0, keepdims=True)
    ones = jnp.ones((8, size), BF)
    for block in range(blocks):
        at = slice(block * CHUNK, (block + 1) * CHUNK)
        resp = (buffer[at] * scale).astype(BF)
        sums[at] = dot(resp, points, (1, 0))
        mass = dot(ones, resp, (1, 1))
        for k in range(CHUNK // lanes):
            totals[block * (CHUNK // lanes) + k] = mass[:, k * lanes : (k + 1) * lanes]

    core = where[1]
    for piece in range(keep.shape[0]):
        block = core * keep.shape[0] + piece
        keep[piece, :lanes, :] = sums[pl.ds(pl.multiple_of(block * lanes, lanes), lanes), :]
        keep[piece, lanes:, :] = jnp.broadcast_to(totals[block, 0:1], (16, lanes))
        block = (1 - core) * keep.shape[0] + piece
        out = sums[pl.ds(pl.multiple_of(block * lanes, lanes), lanes), :]
        send[piece, :lanes, :] = out.astype(BF)
        send[piece, lanes:, :] = pair(totals[block, 0:1]).astype(BF)


def pair(mass):
    high = mass.astype(BF).astype(F32)
    return jnp.concatenate([high, mass - high, jnp.zeros((14, mass.shape[1]), F32)], axis=0)


def cluster(where, product, upper, wide, pieces):
    rows, rank = product.shape
    count = wide.shape[0]
    parcel = (pieces, rank + 16, rank)
    vmem = pl.BlockSpec(memory_space=pltpu.VMEM)
    return pl.pallas_call(
        cluster_body,
        in_specs=[
            pl.BlockSpec(memory_space=pltpu.SMEM), vmem, vmem, pl.BlockSpec(memory_space=pl.ANY),
        ],
        out_shape=[
            jax.ShapeDtypeStruct((rows, rank), BF),
            pltpu.VMEM(parcel, F32),
            jax.ShapeDtypeStruct(parcel, BF),
        ],
        scratch_shapes=[
            pltpu.VMEM((count, rank), F32),
            pltpu.VMEM((count // rank, 8, rank), F32),
            pltpu.VMEM((count, rows), F32),
            pltpu.VMEM(wide.shape, BF),
            pltpu.SemaphoreType.DMA,
        ],
        name="cluster",
    )(where, near(product), near(upper), wide)


def pool_body(keep, got, out):
    lanes = out.shape[2]
    out[:, :lanes, :] = (keep[:, :lanes, :] + got[:, :lanes, :].astype(F32)).astype(BF)
    for piece in range(out.shape[0]):
        tail = got[piece, lanes:, :].astype(F32)
        mass = keep[piece, lanes : lanes + 1, :] + tail[0:1] + tail[1:2]
        out[piece, lanes:, :] = pair(mass).astype(BF)


def mass_body(parts, out):
    lanes = out.shape[1]
    total = jnp.sum(parts[...].astype(F32), axis=0)
    out[:lanes, :] = total[:lanes]
    out[lanes:, :] = jnp.broadcast_to(total[lanes : lanes + 1] + total[lanes + 1 : lanes + 2], (8, lanes))


def centers_body(where, first, second, third, fourth, centroids, out):
    stack = [part[...] for part in (first, second, third, fourth)]
    lanes = out.shape[2]
    total = jnp.zeros_like(stack[0])
    for y in range(SIDE):
        place = (where[0] + SIDE - y) % SIDE
        pick = stack[0]
        for k in range(1, SIDE):
            pick = jnp.where(place == k, stack[k], pick)
        total = total + pick
    column = jnp.transpose(jnp.broadcast_to(total[lanes : lanes + 1], (lanes, lanes)))
    values = ((total[:lanes] + centroids[...].astype(F32)) / (column + 1.0)).astype(BF)
    for copy in range(out.shape[0]):
        out[copy] = values


def join_body(where, mine, theirs, out):
    core = where[1]
    lanes = out.shape[2]
    for piece in range(mine.shape[0]):
        rows = slice(piece * lanes, (piece + 1) * lanes)
        out[core, rows, :] = mine[piece].astype(F32)
        out[1 - core, rows, :] = theirs[piece].astype(F32)


def shards(tiles, tile_list, tile_count, scale_index, scales, panel_start, centroids):
    block_size = tiles.shape[1]
    piece, rank = panel_start.shape
    rows_axis = lax.axis_size("row")
    cols_axis = lax.axis_size("col")
    total_rows = piece * rows_axis * cols_axis
    row_at = lax.axis_index("row")
    col_at = lax.axis_index("col")
    row_blocks = piece * cols_axis // block_size
    col_blocks = piece * rows_axis // block_size
    meta = jnp.concatenate(
        [
            tile_list[:, 0] - row_at * row_blocks,
            tile_list[:, 1] - col_at * col_blocks,
            tile_count,
            jnp.stack([col_at // 2, col_at % 2]).astype(jnp.int32),
        ]
    )
    where = jnp.stack([col_at // 2, col_at % 2, row_at]).astype(jnp.int32)
    table_ids = jnp.arange(scales.shape[0], dtype=jnp.int32)
    weights = jnp.sum(
        jnp.where(scale_index[:, None] == table_ids[None, :], scales[None, :], 0.0), axis=1
    )
    spot = pltpu.VMEM
    square = spot((rank * 3 // 4, rank), F32)
    tall = spot((piece, rank), BF)
    tall_f32 = spot((piece, rank), F32)

    copies_shape = jax.ShapeDtypeStruct((rows_axis, rank, piece), BF)
    panel = panel_start
    gram = None
    for round_index in range(ROUNDS):
        last = round_index + 1 == ROUNDS
        shifted = [shift_col(panel, d, 0) for d in (1, 2, 3)]
        if gram is None:
            *shifted, meta, weights, where = lax.optimization_barrier(
                (*shifted, meta, weights, where)
            )
        else:
            gram = sum_x(gram)
            *shifted, gram = lax.optimization_barrier((*shifted, gram))
            gram = sum_z(gram)
        mine = jnp.stack([panel] + shifted)
        theirs = shift_col(mine, 0, 1)
        partial = tile_call(
            down_body, meta, weights, [mine, theirs], tiles, copies_shape,
            [
                pltpu.VMEM((col_blocks, rank, block_size), F32),
                pltpu.VMEM((block_size, rank), BF),
                pltpu.VMEM((rows_axis, rank, piece), BF),
            ],
        )
        if gram is None:
            parts = lax.all_to_all(partial, "row", 0, 0, tiled=True)
            copies, gram = small_call(reduce_first_body, [copies_shape, square], parts)
        else:
            partial, gram = lax.optimization_barrier((partial, gram))
            parts = lax.all_to_all(partial, "row", 0, 0, tiled=True)
            gram = sum_y(gram)
            upper = factor_of(total_rows, gram, shift_col(gram, 0, 1))
            vmem = pl.BlockSpec(memory_space=pltpu.VMEM)
            copies, gram = pl.pallas_call(
                reduce_down_body,
                in_specs=[pl.BlockSpec(memory_space=pl.ANY), vmem],
                out_shape=[copies_shape, square],
                scratch_shapes=[pltpu.VMEM(parts.shape, BF), pltpu.SemaphoreType.DMA((rows_axis,))],
                name="reduce_down",
            )(parts, near(upper))
        gathered = lax.all_to_all(copies, "row", 0, 0, tiled=True)
        gram = sum_y(gram)
        gram = sum_x(gram + shift_col(gram, 0, 1))
        if last:
            source, _ = lax.optimization_barrier((centroids, copies))
            wide = small_call(
                widen_body, jax.ShapeDtypeStruct((centroids.shape[0], 2 * rank), BF),
                source, far=1,
            )
            owner = (where[1] * rows_axis + where[2]) * rank
            owned = lax.dynamic_slice_in_dim(source, owner, rank, 0)
            gathered, wide, owned = lax.optimization_barrier((gathered, wide, owned))
        gathered, gram = lax.optimization_barrier((gathered, gram))
        grams = ring(gram, lambda v, d: shift_row(v, 0, d))
        keep, send = tile_call(
            up_body, meta, weights, [gathered], tiles,
            [jax.ShapeDtypeStruct((SIDE, piece, rank), F32)] * 2,
            [pltpu.VMEM((row_blocks, block_size, rank), F32)],
        )
        *grams, got = lax.optimization_barrier((*grams, shift_col(send, 0, 1)))
        own, one, two, three = small_call(
            fold_body, [tall_f32, tall, tall, tall], keep, got, where=where,
            far=1,
        )
        *grams, own = lax.optimization_barrier((*grams, own))
        upper = factor_of(total_rows, *grams)
        one, two, three = shift_col(one, 1, 0), shift_col(two, 2, 0), shift_col(three, 3, 0)
        panel, gram = small_call(
            reduce_last_body if last else reduce_up_body,
            [tall_f32 if last else tall, square], own, one, two, three, upper,
        )
    gram = sum_y(gram + shift_col(gram, 0, 1))
    upper = factor_of(total_rows, *ring(sum_x(gram), lambda v, d: shift_row(v, 0, d)))

    panel, keep, send = cluster(where, panel, upper, wide, rows_axis)
    got = shift_col(send, 0, 1)
    packed = small_call(pool_body, spot(send.shape, BF), keep, got)
    parts = lax.all_to_all(packed, "row", 0, 0, tiled=True)
    mass = small_call(mass_body, spot((rank + 8, rank), F32), parts)
    masses = [mass] + [shift_col(mass, d, 0) for d in (1, 2, 3)]
    copies = small_call(
        centers_body, jax.ShapeDtypeStruct((rows_axis, rank, rank), BF), *masses, owned,
        where=where,
    )
    mine = lax.all_to_all(copies, "row", 0, 0, tiled=True)
    theirs = shift_col(mine, 0, 1)
    count = centroids.shape[0]
    centers = small_call(
        join_body, jax.ShapeDtypeStruct((2, count // 2, rank), F32), mine, theirs,
        where=where,
    )
    return (panel, centers.reshape(count, rank))


def solution(mesh):
    return jax.shard_map(
        shards,
        mesh=mesh,
        in_specs=(
            P(("row", "col"), None, None),
            P(("row", "col"), None),
            P(("row", "col")),
            P(("row", "col")),
            P(),
            P(("row", "col"), None),
            P(),
        ),
        out_specs=(P(("row", "col"), None), P()),
        check_vma=False,
    )
```
